32 devices in a mesh: groups: 2 (over x), pts: 16 (over z, y, core).
Axes of the slice: x: 2, y: 2, z: 4, core: 2. Of those that a mesh axis runs over, the one named last changes fastest.
Arguments:
- points: bfloat16 [8192, 512], P(('groups', 'pts')), parts along dimension 0, may hold values from -6 to 6
- labels: int32 [8192], P(('groups', 'pts')), parts along dimension 0, may hold values from 0 to 15
- centres: bfloat16 [32768, 512], P(('groups', 'pts')), parts along dimension 0, may hold values from -6 to 6
- tri_inverse: bfloat16 [32768, 16384], P(('groups', 'pts')), parts along dimension 0, as said below
- beta: bfloat16 [32768, 16], P(('groups', 'pts')), parts along dimension 0, may hold values from -0.01171875 to 0.01171875
- bias: float32 [32], P('groups'), parts along dimension 0, may hold values from -3.2 to -2.2
Outputs:
- gradient: float32 [32768, 16], P(('groups', 'pts')), parts along dimension 0
- logits: float32 [8192, 16], P(('groups', 'pts')), parts along dimension 0
The draws below stay inside these ranges and needn't reach their ends.
There are 2 independent parts, one for each index of `groups`. The reference program is written for one: setup_inputs(seed, part) draws one part's arguments, and reference() takes and returns one part's arrays. A program takes and returns all parts, laid end to end along the dimension named above; each array names one. Nothing has to cross between parts.
Inputs may be any that keep to these rules, and one draw needn't show every extreme that they name: `tri_inverse`: upper triangular: entries below the diagonal are zero; the diagonal lies between 0.6 and 1.4.
All inputs are finite; a program needn't handle non-finite values.
Results may differ from the reference program's by a relative error of at most 0.0039.
Values may be sent and summed in bfloat16 or wider, within the bound.
A program may use at most 128 MiB of HBM per device.

```python
import math
import jax
import jax.numpy as jnp
from jax import lax

CENTRES = 16384
FEATURES = 512
CLASSES = 16
POINTS = 4096


def draw_tri_inverse(key, part):
    key_off, key_diag = jax.random.split(jax.random.fold_in(key, 7))
    offdiag = jax.random.normal(key_off, (CENTRES, CENTRES), jnp.float32) * (0.5 * CENTRES ** (-0.5))
    diagonal = jax.random.uniform(key_diag, (CENTRES,), jnp.float32, 0.6, 1.4)
    row_index = jnp.arange(CENTRES)[:, None]
    col_index = jnp.arange(CENTRES)[None, :]
    result = jnp.where(col_index > row_index, offdiag, 0.0)
    result = jnp.where(col_index == row_index, diagonal[:, None], result)
    return result.astype(jnp.bfloat16)


def place_ends(drawn, stream_key, least, high):
    spot = [jax.random.randint(jax.random.fold_in(stream_key, axis), (), 0, length) for axis, length in enumerate(drawn.shape)]
    main_axis = drawn.shape.index(max(drawn.shape))
    beside = spot[:main_axis] + [(spot[main_axis] + 1) % drawn.shape[main_axis]] + spot[main_axis + 1:]
    return drawn.at[tuple(spot)].set(least).at[tuple(beside)].set(high)


def steps_of(key, shape, shards, low, largest):
    loudness = 1.0
    for axis_at, blocks in shards:
        draws = jax.random.uniform(jax.random.fold_in(jax.random.fold_in(key, 6), axis_at), (blocks,), jnp.float32, low / len(shards), largest / len(shards))
        loudness = loudness * jnp.repeat(jnp.exp(draws), shape[axis_at] // blocks).reshape((-1,) + (1,) * (len(shape) - 1 - axis_at))
    return loudness


def scatter_about(rng, dims, spread, bound, cuts=(), held_as=jnp.bfloat16):
    values = spread * jax.random.normal(rng, dims, jnp.float32)
    if cuts:
        values = values * steps_of(rng, dims, cuts, -0.22, 0.18)
    return jnp.clip(values, -bound, bound).astype(held_as)


def setup_inputs(seed: int = 0, part: int = 0) -> dict:
    key_list = jax.random.split(jax.random.key(seed), 7)
    part_splits = jax.random.split(jax.random.fold_in(key_list[6], part), 7)
    return {
        "points": scatter_about(part_splits[0], (POINTS, FEATURES), 1.0, 6.0, ((0, 16),)),
        "labels": place_ends(jax.random.randint(part_splits[1], (POINTS,), 0, CLASSES), jax.random.fold_in(part_splits[1], 1), 0, CLASSES - 1).astype(jnp.int32),
        "centres": scatter_about(part_splits[2], (CENTRES, FEATURES), 1.0, 6.0, ((0, 16),)),
        "tri_inverse": draw_tri_inverse(jax.random.fold_in(jax.random.fold_in(key_list[6], part), 71), part),
        "beta": scatter_about(part_splits[4], (CENTRES, CLASSES), (16 * CENTRES) ** -0.5, 0.01171875, ((0, 16),)),
        "bias": jnp.clip(jax.random.uniform(part_splits[5], (CLASSES,), jnp.float32, -3.2, -2.2), -3.2, -2.2),
    }


def cube_kernel(point_block, centre_all):
    inner = jnp.dot(point_block, centre_all.T, preferred_element_type=jnp.float32)
    factor = 1.0 / math.sqrt(FEATURES)
    return ((inner * factor + 1.0) ** 3).astype(jnp.bfloat16)

def reference(points, labels, centres, tri_inverse, beta, bias):
    alpha = jnp.dot(tri_inverse, beta, preferred_element_type=jnp.float32).astype(jnp.bfloat16)
    block_size = math.gcd(POINTS, 1024)
    block_count = POINTS // block_size
    point_blocks = points.reshape(block_count, block_size, FEATURES)
    label_blocks = labels.reshape(block_count, block_size)
    classes_row = jnp.arange(CLASSES, dtype=jnp.int32)

    def advance(running, inputs):
        point_block, label_block = inputs
        kernel_tile = cube_kernel(point_block, centres)
        block_logits = jnp.dot(kernel_tile, alpha, preferred_element_type=jnp.float32) + bias[None, :]
        onehot = (label_block[:, None] == classes_row[None, :]).astype(jnp.float32)
        resid = (jax.nn.sigmoid(block_logits) - onehot).astype(jnp.bfloat16)
        update = lax.dot_general(kernel_tile, resid, (((0,), (0,)), ((), ())), preferred_element_type=jnp.float32)
        return (running + update, block_logits)
    grad_sum, logit_blocks = lax.scan(advance, jnp.zeros((CENTRES, CLASSES), jnp.float32), (point_blocks, label_blocks))
    grad_kernel = (grad_sum * (1.0 / math.sqrt(POINTS))).astype(jnp.bfloat16)
    gradient = lax.dot_general(tri_inverse, grad_kernel, (((0,), (0,)), ((), ())), preferred_element_type=jnp.float32)
    return (gradient, logit_blocks.reshape(POINTS, CLASSES))
```

```python
import functools
import math

import jax
import jax.numpy as jnp
from jax import lax
from jax.experimental import pallas as pl
from jax.experimental.pallas import tpu as pltpu
from jax.sharding import PartitionSpec as P

NT = (((1,), (1,)), ((), ()))
NN = (((1,), (0,)), ((), ()))
PIECES = 4


def dot(left, right, dims):
    return lax.dot_general(left, right, dims, preferred_element_type=jnp.float32)


def body(
    n, points, labels, centres, tri, beta, bias, grad_out, logits_out,
    tbuf, pbuf, cbuf, kbuf, bbuf, abuf, asum, lsend, lrecv, rbuf, gsend, grecv, tsend, trecv, total, xsend, xrecv, xown,
    t_sem, own_sem, b_send, b_recv, f_send, p_send, p_recv, c_send, c_recv, a_send, a_recv,
    l_send, l_recv, r_send, r_recv, g_send, g_recv, ts_sem, tr_sem, xs_sem, xr_sem,
):
    chips = n // 2
    depth = chips // 2
    me = lax.axis_index("pts")
    core = lax.rem(me, 2)
    chip = me // 2
    side = lax.rem(chip, 2)
    level = chip // 2
    partner = me + 1 - 2 * core
    size = centres.shape[0]
    factor = 1.0 / math.sqrt(points.shape[1])
    total_points = n * points.shape[0]
    classes = beta.shape[0]

    def remote(src, dst, send, recv, target):
        return pltpu.make_async_remote_copy(
            src_ref=src, dst_ref=dst, send_sem=send, recv_sem=recv,
            device_id={"pts": target}, device_id_type=pl.DeviceIdType.MESH,
        )

    def tri_copy(j):
        start = pl.multiple_of(j * size, size)
        return pltpu.make_async_copy(tri.at[:, pl.ds(start, size)], tbuf.at[j], t_sem.at[j])

    def each(count, fn):
        lax.fori_loop(0, count, lambda i, c: (fn(i), c)[1], 0)

    own_points = pltpu.make_async_copy(points, pbuf.at[chip], own_sem.at[0])
    own_centres = pltpu.make_async_copy(centres, cbuf.at[core], own_sem.at[1])
    own_points.start()
    own_centres.start()

    @functools.partial(each, n)
    def _(j):
        @pl.when(j >= me)
        def _():
            tri_copy(j).start()

    barrier = pltpu.get_barrier_semaphore()

    @functools.partial(each, n)
    def _(q):
        @pl.when(q != me)
        def _():
            pl.semaphore_signal(
                barrier, inc=1, device_id={"pts": q}, device_id_type=pl.DeviceIdType.MESH
            )

    pl.semaphore_wait(barrier, n - 1)

    def beta_send(q):
        block = 2 * q + core
        return remote(beta, bbuf.at[me], b_send.at[q], b_recv.at[me], block)

    def beta_pass(q):
        block = 2 * q + core
        return remote(bbuf.at[block], bbuf.at[block], f_send.at[q], b_recv.at[block], partner)

    own_pass = remote(beta, bbuf.at[me], f_send.at[chip], b_recv.at[me], partner)
    centre_pass = remote(centres, cbuf.at[core], c_send, c_recv, partner)

    @functools.partial(each, chips)
    def _(i):
        q = chips - 1 - i

        @pl.when(q < chip)
        def _():
            beta_send(q).start()

    own_pass.start()
    centre_pass.start()
    bbuf[me] = beta[...]

    def chip_of(lev, sid):
        return 2 * lev + sid

    def inside(lev):
        return (lev >= 0) & (lev < depth)

    piece_rows = points.shape[0] // PIECES

    def point_copy(way, block, piece):
        target = (chip + 2, chip - 2, chip_of(level, 1 - side))[way]
        rows = pbuf.at[block, pl.ds(pl.multiple_of(piece * piece_rows, piece_rows), piece_rows)]
        return remote(
            rows, rows, p_send.at[way, block, piece], p_recv.at[block, piece], 2 * target + core
        )

    def point_sends(lev, piece, act):
        block = chip_of(lev, side)
        for way, wanted in (
            (0, (lev <= level) & (level < depth - 1)),
            (1, (lev >= level) & (level > 0)),
            (2, True),
        ):
            @pl.when(wanted)
            def _():
                act(point_copy(way, block, piece))

    own_points.wait()
    each(PIECES, lambda piece: point_sends(level, piece, lambda c: c.start()))

    def piece_wait(block, piece):
        point_copy(2, block, piece).wait_recv()

    def beta_arrive(q):
        @pl.when(q < chips)
        def _():
            block = 2 * q + core
            remote(beta, bbuf.at[block], b_send.at[0], b_recv.at[block], partner).wait_recv()
            beta_pass(q).start()

    def beta_passed(q):
        block = 2 * q + 1 - core
        remote(beta, bbuf.at[block], b_send.at[0], b_recv.at[block], partner).wait_recv()

    def add_alpha(q):
        @pl.when(q < chips)
        def _():
            beta_arrive(q + 1)
            beta_passed(q)
            tri_copy(2 * q).wait()
            tri_copy(2 * q + 1).wait()
            asum[...] += dot(bbuf[2 * q], tbuf[2 * q], NT) + dot(
                bbuf[2 * q + 1], tbuf[2 * q + 1], NT
            )

    def logit_copy(block):
        return remote(
            lsend.at[block], lrecv.at[chip], l_send.at[block], l_recv.at[chip], 2 * block + core
        )

    alpha_pass = remote(abuf.at[core], abuf.at[core], a_send, a_recv, partner)
    alpha_step = -(-(chips - 1) // PIECES)

    def is_due(block, d):
        gap = block // 2 - level
        reach = d - lax.rem(lax.rem(block, 2) + side, 2)
        earlier = (d == alpha_step) & (gap < reach) & (-gap < reach)
        return (gap == reach) | (-gap == reach) | earlier

    def tile(block):
        def one(half):
            inner = dot(pbuf[block], cbuf[half], NT)
            value = inner * factor + 1.0
            kbuf[block, half] = (value * value * value).astype(jnp.bfloat16)

        each(2, one)

    def step(d):
        @functools.partial(each, PIECES)
        def _(piece):
            @functools.partial(each, 2)
            def _(i):
                lev = level + (2 * i - 1) * d

                @pl.when((d > 0) & inside(lev))
                def _():
                    piece_wait(chip_of(lev, side), piece)
                    point_sends(lev, piece, lambda c: c.start())

            @pl.when((d > 0) & (d <= alpha_step))
            def _():
                add_alpha(chip + (d - 1) * PIECES + piece + 1)

        @pl.when(d == 0)
        def _():
            beta_arrive(chip + 1)
            tri_copy(me).wait()
            asum[...] = dot(bbuf[me], tbuf[me], NT)
            own_centres.wait()

            @pl.when(core == 0)
            def _():
                beta_passed(chip)
                tri_copy(me + 1).wait()
                asum[...] += dot(bbuf[me + 1], tbuf[me + 1], NT)

            @pl.when(core == 1)
            def _():
                beta_passed(chip)

            remote(centres, cbuf.at[1 - core], c_send, c_recv, partner).wait_recv()

        @pl.when(d == alpha_step)
        def _():
            abuf[core] = asum[...].astype(jnp.bfloat16)
            alpha_pass.start()

        @functools.partial(each, 4)
        def _(i):
            sign = 2 * lax.rem(i, 2) - 1
            across = i // 2
            gap = d - across
            lev = level + sign * gap

            @pl.when((gap >= 0) & ((gap > 0) | (sign < 0)) & inside(lev))
            def _():
                block = chip_of(lev, side + across * (1 - 2 * side))

                @pl.when(across == 1)
                def _():
                    each(PIECES, lambda piece: piece_wait(block, piece))

                tile(block)

        @pl.when(d == alpha_step)
        def _():
            remote(abuf.at[core], abuf.at[1 - core], a_send, a_recv, partner).wait_recv()

        @pl.when(d >= alpha_step)
        def _():
            @functools.partial(each, chips)
            def _(block):
                @pl.when(is_due(block, d))
                def _():
                    part = dot(abuf[0], kbuf[block, 0], NT) + dot(abuf[1], kbuf[block, 1], NT)

                    @pl.when(block != chip)
                    def _():
                        lsend[block] = part
                        logit_copy(block).start()

                    @pl.when(block == chip)
                    def _():
                        lrecv[block] = part

    each(depth + 1, step)

    @functools.partial(each, chips)
    def _(q):
        @pl.when(q != chip)
        def _():
            remote(lsend.at[q], lrecv.at[q], l_send.at[q], l_recv.at[q], partner).wait_recv()

    logits = lrecv[0]
    for q in range(1, chips):
        logits = logits + lrecv[q]
    spot = lax.broadcasted_iota(jnp.int32, (classes, classes), 0)
    other = lax.broadcasted_iota(jnp.int32, (classes, classes), 1)
    row = jnp.broadcast_to(bias[...], (classes, classes))
    column = jnp.sum(jnp.where(spot == other, row, 0.0), axis=1, keepdims=True)
    logits = logits + column
    logits_out[...] = logits
    onehot = (labels[...] == lax.broadcasted_iota(jnp.int32, logits.shape, 0)).astype(jnp.float32)
    rbuf[chip] = (jax.nn.sigmoid(logits) - onehot).astype(jnp.bfloat16)

    def resid_copy(q):
        return remote(rbuf.at[chip], rbuf.at[chip], r_send.at[q], r_recv.at[chip], 2 * q + core)

    @functools.partial(each, chips)
    def _(q):
        @pl.when(q != chip)
        def _():
            resid_copy(q).start()

    mid = (depth + 1) // 2
    early = chips // 2

    def turn(i):
        pair = i // 2
        away = pair // 2
        lev = mid - 1 - away + lax.rem(pair, 2) * (2 * away + 1)
        return chip_of(lev, lax.rem(i, 2))

    def resid_wait(q):
        @pl.when(q != chip)
        def _():
            remote(rbuf.at[q], rbuf.at[q], r_send.at[q], r_recv.at[q], partner).wait_recv()

    gsend[...] = jnp.zeros_like(gsend)
    total[...] = jnp.zeros_like(total)

    @functools.partial(each, early)
    def _(i):
        q = turn(i)
        resid_wait(q)
        gsend[...] += dot(rbuf[q], kbuf[q, 1 - core], NN)
        total[...] += dot(rbuf[q], kbuf[q, core], NN)

    @functools.partial(each, chips - early)
    def _(i):
        q = turn(i + early)
        resid_wait(q)
        gsend[...] += dot(rbuf[q], kbuf[q, 1 - core], NN)

    grad_pass = remote(gsend, grecv, g_send, g_recv, partner)
    grad_pass.start()

    @functools.partial(each, chips - early)
    def _(i):
        q = turn(i + early)
        total[...] += dot(rbuf[q], kbuf[q, core], NN)

    mine = total[...]
    grad_pass.wait_recv()
    coeff = ((mine + grecv[...]) * (1.0 / math.sqrt(total_points))).astype(jnp.bfloat16)

    def term_copy(q):
        return remote(tsend.at[q], trecv.at[chip], ts_sem.at[q], tr_sem.at[chip], 2 * q + core)

    def pair_copy(q):
        return remote(xsend.at[q], xrecv.at[q], xs_sem.at[q], xr_sem.at[q], partner)

    def to_pair(q):
        return (q > chip) | ((q == chip) & (core == 0))

    def finish(q):
        pair_copy(q).wait_recv()
        tsend[q] = (xown[q] + xrecv[q]).astype(tsend.dtype)
        term_copy(q).start()

    @functools.partial(each, chips)
    def _(i):
        q = chips - 1 - i

        @pl.when(q > chip)
        def _():
            xsend[q] = dot(coeff, tbuf[2 * q + 1 - core], NN)
            xown[q] = dot(coeff, tbuf[2 * q + core], NN)
            pair_copy(q).start()

        @pl.when((q == chip) & (core == 0))
        def _():
            xsend[q] = dot(coeff, tbuf[2 * q + 1], NN)
            pair_copy(q).start()

        @pl.when(q == chip)
        def _():
            xown[q] = dot(coeff, tbuf[me], NN)

        @pl.when((q >= chip) & (q + 1 < chips))
        def _():
            finish(q + 1)

    total[...] = xown[chip]

    @pl.when(core == 1)
    def _():
        pair_copy(chip).wait_recv()
        total[...] += xrecv[chip]

    @functools.partial(each, chips)
    def _(q):
        @pl.when(q < chip)
        def _():
            remote(tsend.at[q], trecv.at[q], ts_sem.at[q], tr_sem.at[q], partner).wait_recv()
            total[...] += trecv[q].astype(jnp.float32)

    grad_out[...] = total[...]

    @functools.partial(each, chips)
    def _(q):
        @pl.when(q < chip)
        def _():
            beta_send(q).wait_send()

        @pl.when(q > chip)
        def _():
            beta_pass(q).wait_send()

        @pl.when(q != chip)
        def _():
            logit_copy(q).wait_send()
            resid_copy(q).wait_send()

    own_pass.wait_send()
    centre_pass.wait_send()
    alpha_pass.wait_send()
    grad_pass.wait_send()
    each(
        PIECES,
        lambda piece: each(depth, lambda lev: point_sends(lev, piece, lambda c: c.wait_send())),
    )

    @functools.partial(each, chips)
    def _(q):
        @pl.when(to_pair(q))
        def _():
            pair_copy(q).wait_send()

        @pl.when(q > chip)
        def _():
            term_copy(q).wait_send()


def write_out(grad, logits, grad_out, logits_out):
    grad_out[...] = grad[...]
    logits_out[...] = logits[...]


def on_device(points, labels, centres, tri_inverse, beta, bias):
    n = lax.axis_size("pts")
    chips = n // 2
    rows, features = points.shape
    size, classes = beta.shape
    low, full = jnp.bfloat16, jnp.float32
    dma = pltpu.SemaphoreType.DMA
    vmem = pl.BlockSpec(memory_space=pltpu.VMEM)
    hbm = pl.BlockSpec(memory_space=pl.ANY)
    grad_t, logits_t = pl.pallas_call(
        functools.partial(body, n),
        name="falkon_step",
        out_shape=(
            jax.ShapeDtypeStruct((classes, size), full),
            jax.ShapeDtypeStruct((classes, rows), full),
        ),
        in_specs=[hbm, vmem, hbm, hbm, vmem, vmem],
        out_specs=(vmem, vmem),
        scratch_shapes=[
            pltpu.VMEM((n, size, size), low),
            pltpu.VMEM((chips, rows, features), low),
            pltpu.VMEM((2, size, features), low),
            pltpu.VMEM((chips, 2, rows, size), low),
            pltpu.VMEM((n, classes, size), low),
            pltpu.VMEM((2, classes, size), low),
            pltpu.VMEM((classes, size), full),
            pltpu.VMEM((chips, classes, rows), full),
            pltpu.VMEM((chips, classes, rows), full),
            pltpu.VMEM((chips, classes, rows), low),
            pltpu.VMEM((classes, size), full),
            pltpu.VMEM((classes, size), full),
            pltpu.VMEM((chips, classes, size), low),
            pltpu.VMEM((chips, classes, size), low),
            pltpu.VMEM((classes, size), full),
            pltpu.VMEM((chips, classes, size), full),
            pltpu.VMEM((chips, classes, size), full),
            pltpu.VMEM((chips, classes, size), full),
            dma((n,)),
            dma((2,)),
            dma((chips,)),
            dma((n,)),
            dma((chips,)),
            dma((3, chips, PIECES)),
            dma((chips, PIECES)),
            dma, dma, dma, dma,
            dma((chips,)),
            dma((chips,)),
            dma((chips,)),
            dma((chips,)),
            dma, dma,
            dma((chips,)),
            dma((chips,)),
            dma((chips,)),
            dma((chips,)),
        ],
        compiler_params=pltpu.CompilerParams(
            collective_id=0, has_side_effects=True, vmem_limit_bytes=60 * 1024 * 1024
        ),
    )(points, labels[None, :], centres, tri_inverse, beta.T, bias[None, :])
    grad_t, logits_t = pl.pallas_call(
        write_out,
        name="write_out",
        out_shape=(
            jax.ShapeDtypeStruct(grad_t.shape, full),
            jax.ShapeDtypeStruct(logits_t.shape, full),
        ),
        in_specs=[vmem, vmem],
        out_specs=(vmem, vmem),
    )(grad_t, logits_t)
    return grad_t.T, logits_t.T


def solution(mesh):
    return jax.shard_map(
        on_device,
        mesh=mesh,
        in_specs=(
            P(("groups", "pts"), None),
            P(("groups", "pts")),
            P(("groups", "pts"), None),
            P(("groups", "pts"), None),
            P(("groups", "pts"), None),
            P("groups"),
        ),
        out_specs=(P(("groups", "pts"), None), P(("groups", "pts"), None)),
        check_vma=False,
    )
```

```python
import functools
import math

import jax
import jax.numpy as jnp
from jax import lax
from jax.experimental import pallas as pl
from jax.experimental.pallas import tpu as pltpu
from jax.sharding import PartitionSpec as P

NT = (((1,), (1,)), ((), ()))
NN = (((1,), (0,)), ((), ()))
PIECES = 4


def dot(left, right, dims):
    return lax.dot_general(left, right, dims, preferred_element_type=jnp.float32)


def body(
    n, points, labels, centres, tri, beta, bias, grad_out, logits_out,
    tbuf, pbuf, cbuf, kbuf, bbuf, abuf, asum, lsend, lrecv, rbuf, gsend, grecv, tsend, trecv, total, xsend, xrecv, xown,
    t_sem, own_sem, b_send, b_recv, f_send, p_send, p_recv, c_send, c_recv, a_send, a_recv,
    l_send, l_recv, r_send, r_recv, g_send, g_recv, ts_sem, tr_sem, xs_sem, xr_sem,
):
    chips = n // 2
    depth = chips // 2
    me = lax.axis_index("pts")
    core = lax.rem(me, 2)
    chip = me // 2
    side = lax.rem(chip, 2)
    level = chip // 2
    partner = me + 1 - 2 * core
    size = centres.shape[0]
    factor = 1.0 / math.sqrt(points.shape[1])
    total_points = n * points.shape[0]
    classes = beta.shape[0]

    def remote(src, dst, send, recv, target):
        return pltpu.make_async_remote_copy(
            src_ref=src, dst_ref=dst, send_sem=send, recv_sem=recv,
            device_id={"pts": target}, device_id_type=pl.DeviceIdType.MESH,
        )

    def tri_copy(j):
        start = pl.multiple_of(j * size, size)
        return pltpu.make_async_copy(tri.at[:, pl.ds(start, size)], tbuf.at[j], t_sem.at[j])

    def each(count, fn):
        lax.fori_loop(0, count, lambda i, c: (fn(i), c)[1], 0)

    own_points = pltpu.make_async_copy(points, pbuf.at[chip], own_sem.at[0])
    own_centres = pltpu.make_async_copy(centres, cbuf.at[core], own_sem.at[1])
    own_points.start()
    own_centres.start()

    @functools.partial(each, n)
    def _(j):
        @pl.when(j >= me)
        def _():
            tri_copy(j).start()

    barrier = pltpu.get_barrier_semaphore()

    @functools.partial(each, n)
    def _(q):
        @pl.when(q != me)
        def _():
            pl.semaphore_signal(
                barrier, inc=1, device_id={"pts": q}, device_id_type=pl.DeviceIdType.MESH
            )

    pl.semaphore_wait(barrier, n - 1)

    def beta_send(q):
        block = 2 * q + core
        return remote(beta, bbuf.at[me], b_send.at[q], b_recv.at[me], block)

    def beta_pass(q):
        block = 2 * q + core
        return remote(bbuf.at[block], bbuf.at[block], f_send.at[q], b_recv.at[block], partner)

    own_pass = remote(beta, bbuf.at[me], f_send.at[chip], b_recv.at[me], partner)
    centre_pass = remote(centres, cbuf.at[core], c_send, c_recv, partner)

    @functools.partial(each, chips)
    def _(i):
        q = chips - 1 - i

        @pl.when(q < chip)
        def _():
            beta_send(q).start()

    own_pass.start()
    centre_pass.start()
    bbuf[me] = beta[...]

    def chip_of(lev, sid):
        return 2 * lev + sid

    def inside(lev):
        return (lev >= 0) & (lev < depth)

    piece_rows = points.shape[0] // PIECES

    def point_copy(way, block, piece):
        target = (chip + 2, chip - 2, chip_of(level, 1 - side))[way]
        rows = pbuf.at[block, pl.ds(pl.multiple_of(piece * piece_rows, piece_rows), piece_rows)]
        return remote(
            rows, rows, p_send.at[way, block, piece], p_recv.at[block, piece], 2 * target + core
        )

    relay = depth >= 4
    low_end, high_end = relay & (level == 0), relay & (level == depth - 1)
    near_low, near_high = relay & (level == 1), relay & (level == depth - 2)

    def is_split(lev):
        return (low_end & (lev == 1)) | (high_end & (lev == depth - 2))

    def crosses(lev, piece):
        relayed = (near_low & (lev == 0)) | (near_high & (lev == depth - 1))
        return jnp.logical_not(relayed | (is_split(lev) & (piece >= PIECES // 2)))

    def point_sends(lev, piece, act):
        block = chip_of(lev, side)
        for way, wanted in (
            (0, (lev <= level) & (level < depth - 1)),
            (1, (lev >= level) & (level > 0)),
            (2, crosses(lev, piece)),
        ):
            @pl.when(wanted)
            def _():
                act(point_copy(way, block, piece))

    opposite = chip_of(level, 1 - side)

    def relay_sends(piece, act):
        for way, end in ((0, low_end), (1, high_end)):
            @pl.when(end)
            def _():
                act(point_copy(way, opposite, piece))

    def split_sends(piece, act):
        for way, near in ((1, near_low), (0, near_high)):
            @pl.when(near & (piece >= PIECES // 2))
            def _():
                act(point_copy(way, opposite, piece))

    own_points.wait()
    each(PIECES, lambda piece: point_sends(level, piece, lambda c: c.start()))

    def piece_wait(block, piece):
        point_copy(2, block, piece).wait_recv()

    def beta_arrive(q):
        @pl.when(q < chips)
        def _():
            block = 2 * q + core
            remote(beta, bbuf.at[block], b_send.at[0], b_recv.at[block], partner).wait_recv()
            beta_pass(q).start()

    def beta_passed(q):
        block = 2 * q + 1 - core
        remote(beta, bbuf.at[block], b_send.at[0], b_recv.at[block], partner).wait_recv()

    def add_alpha(q):
        @pl.when(q < chips)
        def _():
            beta_arrive(q + 1)
            beta_passed(q)
            tri_copy(2 * q).wait()
            tri_copy(2 * q + 1).wait()
            asum[...] += dot(bbuf[2 * q], tbuf[2 * q], NT) + dot(
                bbuf[2 * q + 1], tbuf[2 * q + 1], NT
            )

    def logit_copy(block):
        return remote(
            lsend.at[block], lrecv.at[chip], l_send.at[block], l_recv.at[chip], 2 * block + core
        )

    alpha_pass = remote(abuf.at[core], abuf.at[core], a_send, a_recv, partner)
    alpha_step = -(-(chips - 1) // PIECES)

    def before_alpha(block):
        gap = block // 2 - level
        across = lax.rem(lax.rem(block, 2) + side, 2)
        reach = alpha_step - across
        split = (across == 1) & is_split(block // 2)
        return (gap < reach) & (-gap < reach) & jnp.logical_not(split)

    def logit_part(block):
        part = dot(abuf[0], kbuf[block, 0], NT) + dot(abuf[1], kbuf[block, 1], NT)

        @pl.when(block != chip)
        def _():
            lsend[block] = part
            logit_copy(block).start()

        @pl.when(block == chip)
        def _():
            lrecv[block] = part

    def tile(block):
        def one(half):
            inner = dot(pbuf[block], cbuf[half], NT)
            value = inner * factor + 1.0
            kbuf[block, half] = (value * value * value).astype(jnp.bfloat16)

        each(2, one)

    def tile_item(stage, item):
        sign = 2 * lax.rem(item, 2) - 1
        late = (stage // depth) * (1 - item // 2)
        across = item // 2 + late
        gap = (stage - item // 2) * (1 - late) + late
        lev = level + sign * gap
        split = (across == 1) & is_split(lev)
        wanted = (gap >= 0) & ((gap > 0) | (sign < 0)) & inside(lev)
        wanted = wanted & (((late == 1) & split) | ((late == 0) & jnp.logical_not(split)))

        @pl.when(wanted)
        def _():
            block = chip_of(lev, side + across * (1 - 2 * side))

            @pl.when((across == 1) & (gap > 0))
            def _():
                each(PIECES, lambda piece: piece_wait(block, piece))

            tile(block)

            @pl.when(stage >= alpha_step)
            def _():
                logit_part(block)

    beta_arrive(chip + 1)
    tri_copy(me).wait()
    asum[...] = dot(bbuf[me], tbuf[me], NT)
    beta_passed(chip)

    @pl.when(core == 0)
    def _():
        tri_copy(me + 1).wait()
        asum[...] += dot(bbuf[me + 1], tbuf[me + 1], NT)

    own_centres.wait()
    remote(centres, cbuf.at[1 - core], c_send, c_recv, partner).wait_recv()

    def step(d):
        @functools.partial(each, PIECES)
        def _(piece):
            @functools.partial(each, 2)
            def _(i):
                lev = level + (2 * i - 1) * d

                @pl.when(inside(lev))
                def _():
                    piece_wait(chip_of(lev, side), piece)
                    point_sends(lev, piece, lambda c: c.start())

            @pl.when(d == 1)
            def _():
                piece_wait(opposite, piece)
                relay_sends(piece, lambda c: c.start())

            @pl.when(d == depth - 2)
            def _():
                @pl.when(piece == PIECES - 1)
                def _():
                    each(PIECES, lambda late: split_sends(late, lambda c: c.start()))

            @pl.when(d <= alpha_step)
            def _():
                add_alpha(chip + (d - 1) * PIECES + piece + 1)

            @pl.when((d == alpha_step) & (piece == PIECES - 1))
            def _():
                abuf[core] = asum[...].astype(jnp.bfloat16)
                alpha_pass.start()

            @pl.when((d == alpha_step + 1) & (piece == 0))
            def _():
                remote(abuf.at[core], abuf.at[1 - core], a_send, a_recv, partner).wait_recv()

            tile_item(d - 1, piece)

            @pl.when(d == alpha_step + 1)
            def _():
                share = -(-chips // PIECES)

                @functools.partial(each, share)
                def _(i):
                    block = piece * share + i

                    @pl.when((block < chips) & before_alpha(block))
                    def _():
                        logit_part(block)

    each(depth + 1, lambda i: step(i + 1))

    @functools.partial(each, chips)
    def _(q):
        @pl.when(q != chip)
        def _():
            remote(lsend.at[q], lrecv.at[q], l_send.at[q], l_recv.at[q], partner).wait_recv()

    logits = lrecv[0]
    for q in range(1, chips):
        logits = logits + lrecv[q]
    spot = lax.broadcasted_iota(jnp.int32, (classes, classes), 0)
    other = lax.broadcasted_iota(jnp.int32, (classes, classes), 1)
    row = jnp.broadcast_to(bias[...], (classes, classes))
    column = jnp.sum(jnp.where(spot == other, row, 0.0), axis=1, keepdims=True)
    logits = logits + column
    logits_out[...] = logits
    onehot = (labels[...] == lax.broadcasted_iota(jnp.int32, logits.shape, 0)).astype(jnp.float32)
    rbuf[chip] = (jax.nn.sigmoid(logits) - onehot).astype(jnp.bfloat16)

    def resid_copy(q):
        return remote(rbuf.at[chip], rbuf.at[chip], r_send.at[q], r_recv.at[chip], 2 * q + core)

    @functools.partial(each, chips)
    def _(q):
        @pl.when(q != chip)
        def _():
            resid_copy(q).start()

    mid = (depth + 1) // 2
    early = chips // 2

    def turn(i):
        pair = i // 2
        away = pair // 2
        lev = mid - 1 - away + lax.rem(pair, 2) * (2 * away + 1)
        return chip_of(lev, lax.rem(i, 2))

    def resid_wait(q):
        @pl.when(q != chip)
        def _():
            remote(rbuf.at[q], rbuf.at[q], r_send.at[q], r_recv.at[q], partner).wait_recv()

    gsend[...] = jnp.zeros_like(gsend)
    total[...] = jnp.zeros_like(total)

    @functools.partial(each, early)
    def _(i):
        q = turn(i)
        resid_wait(q)
        gsend[...] += dot(rbuf[q], kbuf[q, 1 - core], NN)
        total[...] += dot(rbuf[q], kbuf[q, core], NN)

    @functools.partial(each, chips - early)
    def _(i):
        q = turn(i + early)
        resid_wait(q)
        gsend[...] += dot(rbuf[q], kbuf[q, 1 - core], NN)

    grad_pass = remote(gsend, grecv, g_send, g_recv, partner)
    grad_pass.start()

    @functools.partial(each, chips - early)
    def _(i):
        q = turn(i + early)
        total[...] += dot(rbuf[q], kbuf[q, core], NN)

    mine = total[...]
    grad_pass.wait_recv()
    coeff = ((mine + grecv[...]) * (1.0 / math.sqrt(total_points))).astype(jnp.bfloat16)

    def term_copy(q):
        return remote(tsend.at[q], trecv.at[chip], ts_sem.at[q], tr_sem.at[chip], 2 * q + core)

    def pair_copy(q):
        return remote(xsend.at[q], xrecv.at[q], xs_sem.at[q], xr_sem.at[q], partner)

    def to_pair(q):
        return (q > chip) | ((q == chip) & (core == 0))

    def finish(q):
        pair_copy(q).wait_recv()
        tsend[q] = (xown[q] + xrecv[q]).astype(tsend.dtype)
        term_copy(q).start()

    @functools.partial(each, chips)
    def _(i):
        q = chips - 1 - i

        @pl.when(q > chip)
        def _():
            xsend[q] = dot(coeff, tbuf[2 * q + 1 - core], NN)
            xown[q] = dot(coeff, tbuf[2 * q + core], NN)
            pair_copy(q).start()

        @pl.when((q == chip) & (core == 0))
        def _():
            xsend[q] = dot(coeff, tbuf[2 * q + 1], NN)
            pair_copy(q).start()

        @pl.when(q == chip)
        def _():
            xown[q] = dot(coeff, tbuf[me], NN)

        @pl.when((q >= chip) & (q + 1 < chips))
        def _():
            finish(q + 1)

    total[...] = xown[chip]

    @pl.when(core == 1)
    def _():
        pair_copy(chip).wait_recv()
        total[...] += xrecv[chip]

    @functools.partial(each, chips)
    def _(q):
        @pl.when(q < chip)
        def _():
            remote(tsend.at[q], trecv.at[q], ts_sem.at[q], tr_sem.at[q], partner).wait_recv()
            total[...] += trecv[q].astype(jnp.float32)

    grad_out[...] = total[...]

    @functools.partial(each, chips)
    def _(q):
        @pl.when(q < chip)
        def _():
            beta_send(q).wait_send()

        @pl.when(q > chip)
        def _():
            beta_pass(q).wait_send()

        @pl.when(q != chip)
        def _():
            logit_copy(q).wait_send()
            resid_copy(q).wait_send()

    own_pass.wait_send()
    centre_pass.wait_send()
    alpha_pass.wait_send()
    grad_pass.wait_send()
    @functools.partial(each, PIECES)
    def _(piece):
        each(depth, lambda lev: point_sends(lev, piece, lambda c: c.wait_send()))
        relay_sends(piece, lambda c: c.wait_send())
        split_sends(piece, lambda c: c.wait_send())


    @functools.partial(each, chips)
    def _(q):
        @pl.when(to_pair(q))
        def _():
            pair_copy(q).wait_send()

        @pl.when(q > chip)
        def _():
            term_copy(q).wait_send()


def write_out(grad, logits, grad_out, logits_out):
    grad_out[...] = grad[...]
    logits_out[...] = logits[...]


def on_device(points, labels, centres, tri_inverse, beta, bias):
    n = lax.axis_size("pts")
    chips = n // 2
    rows, features = points.shape
    size, classes = beta.shape
    low, full = jnp.bfloat16, jnp.float32
    dma = pltpu.SemaphoreType.DMA
    vmem = pl.BlockSpec(memory_space=pltpu.VMEM)
    hbm = pl.BlockSpec(memory_space=pl.ANY)
    grad_t, logits_t = pl.pallas_call(
        functools.partial(body, n),
        name="falkon_step",
        out_shape=(
            jax.ShapeDtypeStruct((classes, size), full),
            jax.ShapeDtypeStruct((classes, rows), full),
        ),
        in_specs=[hbm, vmem, hbm, hbm, vmem, vmem],
        out_specs=(vmem, vmem),
        scratch_shapes=[
            pltpu.VMEM((n, size, size), low),
            pltpu.VMEM((chips, rows, features), low),
            pltpu.VMEM((2, size, features), low),
            pltpu.VMEM((chips, 2, rows, size), low),
            pltpu.VMEM((n, classes, size), low),
            pltpu.VMEM((2, classes, size), low),
            pltpu.VMEM((classes, size), full),
            pltpu.VMEM((chips, classes, rows), full),
            pltpu.VMEM((chips, classes, rows), full),
            pltpu.VMEM((chips, classes, rows), low),
            pltpu.VMEM((classes, size), full),
            pltpu.VMEM((classes, size), full),
            pltpu.VMEM((chips, classes, size), low),
            pltpu.VMEM((chips, classes, size), low),
            pltpu.VMEM((classes, size), full),
            pltpu.VMEM((chips, classes, size), full),
            pltpu.VMEM((chips, classes, size), full),
            pltpu.VMEM((chips, classes, size), full),
            dma((n,)),
            dma((2,)),
            dma((chips,)),
            dma((n,)),
            dma((chips,)),
            dma((3, chips, PIECES)),
            dma((chips, PIECES)),
            dma, dma, dma, dma,
            dma((chips,)),
            dma((chips,)),
            dma((chips,)),
            dma((chips,)),
            dma, dma,
            dma((chips,)),
            dma((chips,)),
            dma((chips,)),
            dma((chips,)),
        ],
        compiler_params=pltpu.CompilerParams(
            collective_id=0, has_side_effects=True, vmem_limit_bytes=60 * 1024 * 1024
        ),
    )(points, labels[None, :], centres, tri_inverse, beta.T, bias[None, :])
    grad_t, logits_t = pl.pallas_call(
        write_out,
        name="write_out",
        out_shape=(
            jax.ShapeDtypeStruct(grad_t.shape, full),
            jax.ShapeDtypeStruct(logits_t.shape, full),
        ),
        in_specs=[vmem, vmem],
        out_specs=(vmem, vmem),
    )(grad_t, logits_t)
    return grad_t.T, logits_t.T


def solution(mesh):
    return jax.shard_map(
        on_device,
        mesh=mesh,
        in_specs=(
            P(("groups", "pts"), None),
            P(("groups", "pts")),
            P(("groups", "pts"), None),
            P(("groups", "pts"), None),
            P(("groups", "pts"), None),
            P("groups"),
        ),
        out_specs=(P(("groups", "pts"), None), P(("groups", "pts"), None)),
        check_vma=False,
    )
```

```python
import functools
import math

import jax
import jax.numpy as jnp
from jax import lax
from jax.experimental import pallas as pl
from jax.experimental.pallas import tpu as pltpu
from jax.sharding import PartitionSpec as P

NT = (((1,), (1,)), ((), ()))
NN = (((1,), (0,)), ((), ()))
PIECES = 4


def dot(left, right, dims):
    return lax.dot_general(left, right, dims, preferred_element_type=jnp.float32)


def body(
    n, points, labels, centres, tri, beta, bias, grad_out, logits_out,
    tbuf, pbuf, cbuf, kbuf, bbuf, abuf, asum, lsend, lrecv, rbuf, gsend, grecv, tsend, trecv, total, xsend, xrecv, xown,
    t_sem, own_sem, b_send, b_recv, f_send, p_send, p_recv, c_send, c_recv, a_send, a_recv,
    l_send, l_recv, r_send, r_recv, g_send, g_recv, ts_sem, tr_sem, xs_sem, xr_sem,
):
    chips = n // 2
    depth = chips // 2
    me = lax.axis_index("pts")
    core = lax.rem(me, 2)
    chip = me // 2
    side = lax.rem(chip, 2)
    level = chip // 2
    partner = me + 1 - 2 * core
    size = centres.shape[0]
    factor = 1.0 / math.sqrt(points.shape[1])
    total_points = n * points.shape[0]
    classes = beta.shape[0]

    def remote(src, dst, send, recv, target):
        return pltpu.make_async_remote_copy(
            src_ref=src, dst_ref=dst, send_sem=send, recv_sem=recv,
            device_id={"pts": target}, device_id_type=pl.DeviceIdType.MESH,
        )

    def tri_copy(j):
        start = pl.multiple_of(j * size, size)
        return pltpu.make_async_copy(tri.at[:, pl.ds(start, size)], tbuf.at[j], t_sem.at[j])

    def each(count, fn):
        lax.fori_loop(0, count, lambda i, c: (fn(i), c)[1], 0)

    own_points = pltpu.make_async_copy(points, pbuf.at[chip], own_sem.at[0])
    own_centres = pltpu.make_async_copy(centres, cbuf.at[core], own_sem.at[1])
    own_points.start()
    own_centres.start()

    @functools.partial(each, n)
    def _(j):
        @pl.when(j >= me)
        def _():
            tri_copy(j).start()

    barrier = pltpu.get_barrier_semaphore()

    @functools.partial(each, n)
    def _(q):
        @pl.when(q != me)
        def _():
            pl.semaphore_signal(
                barrier, inc=1, device_id={"pts": q}, device_id_type=pl.DeviceIdType.MESH
            )

    pl.semaphore_wait(barrier, n - 1)

    def chip_of(lev, sid):
        return 2 * lev + sid

    def inside(lev):
        return (lev >= 0) & (lev < depth)

    def beta_copy(way, q):
        block = 2 * q + core
        target = (chip - 2, chip_of(level, 1 - side))[way]
        return remote(
            bbuf.at[block], bbuf.at[block], b_send.at[way, q], b_recv.at[block], 2 * target + core
        )

    def beta_sends(lev, act):
        q = chip_of(lev, side)

        @pl.when(level > 0)
        def _():
            act(beta_copy(0, q))

        @pl.when((lev > level) | (side == 1))
        def _():
            act(beta_copy(1, q))

    def beta_pass(q):
        block = 2 * q + core
        return remote(bbuf.at[block], bbuf.at[block], f_send.at[q], b_recv.at[block], partner)

    own_pass = beta_pass(chip)
    centre_pass = remote(centres, cbuf.at[core], c_send, c_recv, partner)

    bbuf[me] = beta[...]
    beta_sends(level, lambda c: c.start())
    own_pass.start()
    centre_pass.start()

    piece_rows = points.shape[0] // PIECES

    def point_copy(way, block, piece):
        target = (chip + 2, chip - 2, chip_of(level, 1 - side))[way]
        rows = pbuf.at[block, pl.ds(pl.multiple_of(piece * piece_rows, piece_rows), piece_rows)]
        return remote(
            rows, rows, p_send.at[way, block, piece], p_recv.at[block, piece], 2 * target + core
        )

    relay = depth >= 4
    low_end, high_end = relay & (level == 0), relay & (level == depth - 1)
    near_low, near_high = relay & (level == 1), relay & (level == depth - 2)

    def is_split(lev):
        return (low_end & (lev == 1)) | (high_end & (lev == depth - 2))

    def crosses(lev, piece):
        relayed = (near_low & (lev == 0)) | (near_high & (lev == depth - 1))
        return jnp.logical_not(relayed | (is_split(lev) & (piece >= PIECES // 2)))

    def point_sends(lev, piece, act):
        block = chip_of(lev, side)
        for way, wanted in (
            (0, (lev <= level) & (level < depth - 1)),
            (1, (lev >= level) & (level > 0)),
            (2, crosses(lev, piece)),
        ):
            @pl.when(wanted)
            def _():
                act(point_copy(way, block, piece))

    opposite = chip_of(level, 1 - side)

    def relay_sends(piece, act):
        for way, end in ((0, low_end), (1, high_end)):
            @pl.when(end)
            def _():
                act(point_copy(way, opposite, piece))

    def split_sends(piece, act):
        for way, near in ((1, near_low), (0, near_high)):
            @pl.when(near & (piece >= PIECES // 2))
            def _():
                act(point_copy(way, opposite, piece))

    own_points.wait()
    each(PIECES, lambda piece: point_sends(level, piece, lambda c: c.start()))

    def piece_wait(block, piece):
        point_copy(2, block, piece).wait_recv()

    def beta_arrive(q):
        beta_copy(1, q).wait_recv()
        beta_pass(q).start()

    def beta_passed(q):
        block = 2 * q + 1 - core
        remote(
            bbuf.at[block], bbuf.at[block], f_send.at[q], b_recv.at[block], partner
        ).wait_recv()

    def add_alpha(q):
        beta_passed(q)
        tri_copy(2 * q).wait()
        tri_copy(2 * q + 1).wait()
        asum[...] += dot(bbuf[2 * q], tbuf[2 * q], NT) + dot(bbuf[2 * q + 1], tbuf[2 * q + 1], NT)

    def alpha_slot(slot):
        reach = (slot + 1) // 2
        odd = lax.rem(slot, 2) == 1
        above = level + slot // 2 + 1
        own = level + reach
        across = level + reach - 1
        wanted = (across < depth) & ((reach > 1) | (side == 0))

        @pl.when(jnp.logical_not(odd) & (above < depth))
        def _():
            beta_arrive(chip_of(above, side))
            beta_sends(above, lambda c: c.start())

        @pl.when(jnp.logical_not(odd) & (level + slot // 2 < depth) & ((slot > 0) | (side == 0)))
        def _():
            beta_arrive(chip_of(level + slot // 2, 1 - side))

        @pl.when(odd & (own < depth))
        def _():
            add_alpha(chip_of(own, side))

        @pl.when(odd & wanted)
        def _():
            add_alpha(chip_of(across, 1 - side))

    def logit_copy(block):
        return remote(
            lsend.at[block], lrecv.at[chip], l_send.at[block], l_recv.at[chip], 2 * block + core
        )

    alpha_pass = remote(abuf.at[core], abuf.at[core], a_send, a_recv, partner)
    alpha_step = (2 * depth - 1) // PIECES + 1

    def before_alpha(block):
        gap = block // 2 - level
        across = lax.rem(lax.rem(block, 2) + side, 2)
        reach = alpha_step - across
        split = (across == 1) & is_split(block // 2)
        return (gap < reach) & (-gap < reach) & jnp.logical_not(split)

    def logit_part(block):
        part = dot(abuf[0], kbuf[block, 0], NT) + dot(abuf[1], kbuf[block, 1], NT)

        @pl.when(block != chip)
        def _():
            lsend[block] = part
            logit_copy(block).start()

        @pl.when(block == chip)
        def _():
            lrecv[block] = part

    def tile(block):
        def one(half):
            inner = dot(pbuf[block], cbuf[half], NT)
            value = inner * factor + 1.0
            kbuf[block, half] = (value * value * value).astype(jnp.bfloat16)

        each(2, one)

    def tile_item(stage, item):
        sign = 2 * lax.rem(item, 2) - 1
        late = (stage // depth) * (1 - item // 2)
        across = item // 2 + late
        gap = (stage - item // 2) * (1 - late) + late
        lev = level + sign * gap
        split = (across == 1) & is_split(lev)
        wanted = (gap >= 0) & ((gap > 0) | (sign < 0)) & inside(lev)
        wanted = wanted & (((late == 1) & split) | ((late == 0) & jnp.logical_not(split)))

        @pl.when(wanted)
        def _():
            block = chip_of(lev, side + across * (1 - 2 * side))

            @pl.when((across == 1) & (gap > 0))
            def _():
                each(PIECES, lambda piece: piece_wait(block, piece))

            tile(block)

            @pl.when(stage >= alpha_step)
            def _():
                logit_part(block)

    tri_copy(me).wait()
    asum[...] = dot(bbuf[me], tbuf[me], NT)
    beta_passed(chip)

    @pl.when(core == 0)
    def _():
        tri_copy(me + 1).wait()
        asum[...] += dot(bbuf[me + 1], tbuf[me + 1], NT)

    own_centres.wait()
    remote(centres, cbuf.at[1 - core], c_send, c_recv, partner).wait_recv()

    def step(d):
        @functools.partial(each, PIECES)
        def _(piece):
            @functools.partial(each, 2)
            def _(i):
                lev = level + (2 * i - 1) * d

                @pl.when(inside(lev))
                def _():
                    piece_wait(chip_of(lev, side), piece)
                    point_sends(lev, piece, lambda c: c.start())

            @pl.when(d == 1)
            def _():
                piece_wait(opposite, piece)
                relay_sends(piece, lambda c: c.start())

            @pl.when(d == depth - 2)
            def _():
                @pl.when(piece == PIECES - 1)
                def _():
                    each(PIECES, lambda late: split_sends(late, lambda c: c.start()))

            @pl.when(d <= alpha_step)
            def _():
                alpha_slot((d - 1) * PIECES + piece)

            @pl.when((d == alpha_step) & (piece == PIECES - 1))
            def _():
                abuf[core] = asum[...].astype(jnp.bfloat16)
                alpha_pass.start()

            @pl.when((d == alpha_step + 1) & (piece == 0))
            def _():
                remote(abuf.at[core], abuf.at[1 - core], a_send, a_recv, partner).wait_recv()

            tile_item(d - 1, piece)

            @pl.when(d == alpha_step + 1)
            def _():
                share = -(-chips // PIECES)

                @functools.partial(each, share)
                def _(i):
                    block = piece * share + i

                    @pl.when((block < chips) & before_alpha(block))
                    def _():
                        logit_part(block)

    each(depth + 1, lambda i: step(i + 1))

    @functools.partial(each, chips)
    def _(q):
        @pl.when(q != chip)
        def _():
            remote(lsend.at[q], lrecv.at[q], l_send.at[q], l_recv.at[q], partner).wait_recv()

    logits = lrecv[0]
    for q in range(1, chips):
        logits = logits + lrecv[q]
    spot = lax.broadcasted_iota(jnp.int32, (classes, classes), 0)
    other = lax.broadcasted_iota(jnp.int32, (classes, classes), 1)
    row = jnp.broadcast_to(bias[...], (classes, classes))
    column = jnp.sum(jnp.where(spot == other, row, 0.0), axis=1, keepdims=True)
    logits = logits + column
    logits_out[...] = logits
    onehot = (labels[...] == lax.broadcasted_iota(jnp.int32, logits.shape, 0)).astype(jnp.float32)
    rbuf[chip] = (jax.nn.sigmoid(logits) - onehot).astype(jnp.bfloat16)

    def resid_copy(q):
        return remote(rbuf.at[chip], rbuf.at[chip], r_send.at[q], r_recv.at[chip], 2 * q + core)

    @functools.partial(each, chips)
    def _(q):
        @pl.when(q != chip)
        def _():
            resid_copy(q).start()

    mid = (depth + 1) // 2
    early = chips // 2

    def turn(i):
        pair = i // 2
        away = pair // 2
        lev = mid - 1 - away + lax.rem(pair, 2) * (2 * away + 1)
        return chip_of(lev, lax.rem(i, 2))

    def resid_wait(q):
        @pl.when(q != chip)
        def _():
            remote(rbuf.at[q], rbuf.at[q], r_send.at[q], r_recv.at[q], partner).wait_recv()

    gsend[...] = jnp.zeros_like(gsend)
    total[...] = jnp.zeros_like(total)

    @functools.partial(each, early)
    def _(i):
        q = turn(i)
        resid_wait(q)
        gsend[...] += dot(rbuf[q], kbuf[q, 1 - core], NN)
        total[...] += dot(rbuf[q], kbuf[q, core], NN)

    @functools.partial(each, chips - early)
    def _(i):
        q = turn(i + early)
        resid_wait(q)
        gsend[...] += dot(rbuf[q], kbuf[q, 1 - core], NN)

    grad_pass = remote(gsend, grecv, g_send, g_recv, partner)
    grad_pass.start()

    @functools.partial(each, chips - early)
    def _(i):
        q = turn(i + early)
        total[...] += dot(rbuf[q], kbuf[q, core], NN)

    mine = total[...]
    grad_pass.wait_recv()
    coeff = ((mine + grecv[...]) * (1.0 / math.sqrt(total_points))).astype(jnp.bfloat16)

    def term_copy(q):
        return remote(tsend.at[q], trecv.at[chip], ts_sem.at[q], tr_sem.at[chip], 2 * q + core)

    def pair_copy(q):
        return remote(xsend.at[q], xrecv.at[q], xs_sem.at[q], xr_sem.at[q], partner)

    def to_pair(q):
        return (q > chip) | ((q == chip) & (core == 0))

    def finish(q):
        pair_copy(q).wait_recv()
        tsend[q] = (xown[q] + xrecv[q]).astype(tsend.dtype)
        term_copy(q).start()

    @functools.partial(each, chips)
    def _(i):
        q = chips - 1 - i

        @pl.when(q > chip)
        def _():
            xsend[q] = dot(coeff, tbuf[2 * q + 1 - core], NN)
            xown[q] = dot(coeff, tbuf[2 * q + core], NN)
            pair_copy(q).start()

        @pl.when((q == chip) & (core == 0))
        def _():
            xsend[q] = dot(coeff, tbuf[2 * q + 1], NN)
            pair_copy(q).start()

        @pl.when(q == chip)
        def _():
            xown[q] = dot(coeff, tbuf[me], NN)

        @pl.when((q >= chip) & (q + 1 < chips))
        def _():
            finish(q + 1)

    total[...] = xown[chip]

    @pl.when(core == 1)
    def _():
        pair_copy(chip).wait_recv()
        total[...] += xrecv[chip]

    @functools.partial(each, chips)
    def _(q):
        @pl.when(q < chip)
        def _():
            remote(tsend.at[q], trecv.at[q], ts_sem.at[q], tr_sem.at[q], partner).wait_recv()
            total[...] += trecv[q].astype(jnp.float32)

    grad_out[...] = total[...]

    @functools.partial(each, chips)
    def _(q):
        @pl.when(q > chip)
        def _():
            beta_pass(q).wait_send()

        @pl.when(q != chip)
        def _():
            logit_copy(q).wait_send()
            resid_copy(q).wait_send()

    @functools.partial(each, depth)
    def _(lev):
        @pl.when(lev >= level)
        def _():
            beta_sends(lev, lambda c: c.wait_send())

    own_pass.wait_send()
    centre_pass.wait_send()
    alpha_pass.wait_send()
    grad_pass.wait_send()
    @functools.partial(each, PIECES)
    def _(piece):
        each(depth, lambda lev: point_sends(lev, piece, lambda c: c.wait_send()))
        relay_sends(piece, lambda c: c.wait_send())
        split_sends(piece, lambda c: c.wait_send())


    @functools.partial(each, chips)
    def _(q):
        @pl.when(to_pair(q))
        def _():
            pair_copy(q).wait_send()

        @pl.when(q > chip)
        def _():
            term_copy(q).wait_send()


def write_out(grad, logits, grad_out, logits_out):
    grad_out[...] = grad[...]
    logits_out[...] = logits[...]


def on_device(points, labels, centres, tri_inverse, beta, bias):
    n = lax.axis_size("pts")
    chips = n // 2
    rows, features = points.shape
    size, classes = beta.shape
    low, full = jnp.bfloat16, jnp.float32
    dma = pltpu.SemaphoreType.DMA
    vmem = pl.BlockSpec(memory_space=pltpu.VMEM)
    hbm = pl.BlockSpec(memory_space=pl.ANY)
    grad_t, logits_t = pl.pallas_call(
        functools.partial(body, n),
        name="falkon_step",
        out_shape=(
            jax.ShapeDtypeStruct((classes, size), full),
            jax.ShapeDtypeStruct((classes, rows), full),
        ),
        in_specs=[hbm, vmem, hbm, hbm, vmem, vmem],
        out_specs=(vmem, vmem),
        scratch_shapes=[
            pltpu.VMEM((n, size, size), low),
            pltpu.VMEM((chips, rows, features), low),
            pltpu.VMEM((2, size, features), low),
            pltpu.VMEM((chips, 2, rows, size), low),
            pltpu.VMEM((n, classes, size), low),
            pltpu.VMEM((2, classes, size), low),
            pltpu.VMEM((classes, size), full),
            pltpu.VMEM((chips, classes, rows), full),
            pltpu.VMEM((chips, classes, rows), full),
            pltpu.VMEM((chips, classes, rows), low),
            pltpu.VMEM((classes, size), full),
            pltpu.VMEM((classes, size), full),
            pltpu.VMEM((chips, classes, size), low),
            pltpu.VMEM((chips, classes, size), low),
            pltpu.VMEM((classes, size), full),
            pltpu.VMEM((chips, classes, size), full),
            pltpu.VMEM((chips, classes, size), full),
            pltpu.VMEM((chips, classes, size), full),
            dma((n,)),
            dma((2,)),
            dma((2, chips)),
            dma((n,)),
            dma((chips,)),
            dma((3, chips, PIECES)),
            dma((chips, PIECES)),
            dma, dma, dma, dma,
            dma((chips,)),
            dma((chips,)),
            dma((chips,)),
            dma((chips,)),
            dma, dma,
            dma((chips,)),
            dma((chips,)),
            dma((chips,)),
            dma((chips,)),
        ],
        compiler_params=pltpu.CompilerParams(
            collective_id=0, has_side_effects=True, vmem_limit_bytes=60 * 1024 * 1024
        ),
    )(points, labels[None, :], centres, tri_inverse, beta.T, bias[None, :])
    grad_t, logits_t = pl.pallas_call(
        write_out,
        name="write_out",
        out_shape=(
            jax.ShapeDtypeStruct(grad_t.shape, full),
            jax.ShapeDtypeStruct(logits_t.shape, full),
        ),
        in_specs=[vmem, vmem],
        out_specs=(vmem, vmem),
    )(grad_t, logits_t)
    return grad_t.T, logits_t.T


def solution(mesh):
    return jax.shard_map(
        on_device,
        mesh=mesh,
        in_specs=(
            P(("groups", "pts"), None),
            P(("groups", "pts")),
            P(("groups", "pts"), None),
            P(("groups", "pts"), None),
            P(("groups", "pts"), None),
            P("groups"),
        ),
        out_specs=(P(("groups", "pts"), None), P(("groups", "pts"), None)),
        check_vma=False,
    )
```

```python
import functools
import math

import jax
import jax.numpy as jnp
from jax import lax
from jax.experimental import pallas as pl
from jax.experimental.pallas import tpu as pltpu
from jax.sharding import PartitionSpec as P

NT = (((1,), (1,)), ((), ()))
NN = (((1,), (0,)), ((), ()))
PIECES = 2


def dot(left, right, dims):
    return lax.dot_general(left, right, dims, preferred_element_type=jnp.float32)


def body(
    n, points, labels, centres, tri, beta, bias, grad_out, logits_out,
    tbuf, pbuf, cbuf, kbuf, bbuf, abuf, asum, lsend, lrecv, rbuf, gsend, grecv, tsend, trecv, total, xsend, xrecv, xown,
    t_sem, own_sem, b_send, b_recv, f_send, p_send, p_recv, c_send, c_recv, a_send, a_recv,
    l_send, l_recv, r_send, r_recv, g_send, g_recv, ts_sem, tr_sem, xs_sem, xr_sem,
):
    chips = n // 2
    depth = chips // 2
    me = lax.axis_index("pts")
    core = lax.rem(me, 2)
    chip = me // 2
    side = lax.rem(chip, 2)
    level = chip // 2
    partner = me + 1 - 2 * core
    size = centres.shape[0]
    factor = 1.0 / math.sqrt(points.shape[1])
    total_points = n * points.shape[0]
    classes = beta.shape[0]

    def remote(src, dst, send, recv, target):
        return pltpu.make_async_remote_copy(
            src_ref=src, dst_ref=dst, send_sem=send, recv_sem=recv,
            device_id={"pts": target}, device_id_type=pl.DeviceIdType.MESH,
        )

    def tri_copy(j):
        start = pl.multiple_of(j * size, size)
        return pltpu.make_async_copy(tri.at[:, pl.ds(start, size)], tbuf.at[j], t_sem.at[j])

    def each(count, fn):
        lax.fori_loop(0, count, lambda i, c: (fn(i), c)[1], 0)

    own_points = pltpu.make_async_copy(points, pbuf.at[chip], own_sem.at[0])
    own_centres = pltpu.make_async_copy(centres, cbuf.at[core], own_sem.at[1])
    own_points.start()
    own_centres.start()

    @functools.partial(each, n)
    def _(j):
        @pl.when(j >= me)
        def _():
            tri_copy(j).start()

    barrier = pltpu.get_barrier_semaphore()

    @functools.partial(each, n)
    def _(q):
        @pl.when(q != me)
        def _():
            pl.semaphore_signal(
                barrier, inc=1, device_id={"pts": q}, device_id_type=pl.DeviceIdType.MESH
            )

    pl.semaphore_wait(barrier, n - 1)

    def beta_send(q):
        block = 2 * q + core
        return remote(beta, bbuf.at[me], b_send.at[q], b_recv.at[me], block)

    def beta_pass(q):
        block = 2 * q + core
        return remote(bbuf.at[block], bbuf.at[block], f_send.at[q], b_recv.at[block], partner)

    def beta_direct(q):
        return (q < chip) & ((lax.rem(q, 2) == side) | (q == chip - side))

    def beta_cross(lev):
        q = 2 * lev + side
        block = 2 * q + core
        target = 2 * (2 * level + 1 - side) + core
        return remote(bbuf.at[block], bbuf.at[block], b_send.at[q], b_recv.at[block], target)

    own_pass = remote(beta, bbuf.at[me], f_send.at[chip], b_recv.at[me], partner)
    centre_pass = remote(centres, cbuf.at[core], c_send, c_recv, partner)

    def chip_of(lev, sid):
        return 2 * lev + sid

    def inside(lev):
        return (lev >= 0) & (lev < depth)

    piece_rows = points.shape[0] // PIECES

    def point_copy(way, block, piece):
        target = (chip + 2, chip - 2, chip_of(level, 1 - side))[way]
        rows = pbuf.at[block, pl.ds(pl.multiple_of(piece * piece_rows, piece_rows), piece_rows)]
        return remote(
            rows, rows, p_send.at[way, block, piece], p_recv.at[block, piece], 2 * target + core
        )

    @functools.partial(each, chips)
    def _(i):
        q = chips - 1 - i

        @pl.when(beta_direct(q))
        def _():
            beta_send(q).start()

    own_pass.start()
    centre_pass.start()
    bbuf[me] = beta[...]
    relay = depth >= 4
    low_end, high_end = relay & (level == 0), relay & (level == depth - 1)
    near_low, near_high = relay & (level == 1), relay & (level == depth - 2)

    def is_split(lev):
        return (low_end & (lev == 1)) | (high_end & (lev == depth - 2))

    def crosses(lev, piece):
        relayed = (near_low & (lev == 0)) | (near_high & (lev == depth - 1))
        return jnp.logical_not(relayed | (is_split(lev) & (piece >= PIECES // 2)))

    def point_sends(lev, piece, act):
        block = chip_of(lev, side)
        for way, wanted in (
            (0, (lev <= level) & (level < depth - 1)),
            (1, (lev >= level) & (level > 0)),
            (2, crosses(lev, piece)),
        ):
            @pl.when(wanted)
            def _():
                act(point_copy(way, block, piece))

    opposite = chip_of(level, 1 - side)

    def relay_sends(piece, act):
        for way, end in ((0, low_end), (1, high_end)):
            @pl.when(end)
            def _():
                act(point_copy(way, opposite, piece))

    def split_sends(piece, act):
        for way, near in ((1, near_low), (0, near_high)):
            @pl.when(near & (piece >= PIECES // 2))
            def _():
                act(point_copy(way, opposite, piece))

    own_points.wait()
    each(PIECES, lambda piece: point_sends(level, piece, lambda c: c.start()))

    def piece_wait(block, piece):
        point_copy(2, block, piece).wait_recv()

    def beta_wait(q):
        block = 2 * q + core
        remote(beta, bbuf.at[block], b_send.at[0], b_recv.at[block], partner).wait_recv()

    def beta_arrive(q):
        beta_wait(q)
        beta_pass(q).start()

    def beta_passed(q):
        block = 2 * q + 1 - core
        remote(beta, bbuf.at[block], b_send.at[0], b_recv.at[block], partner).wait_recv()

    def add_alpha(q):
        beta_passed(q)
        tri_copy(2 * q).wait()
        tri_copy(2 * q + 1).wait()
        asum[...] += dot(bbuf[2 * q], tbuf[2 * q], NT) + dot(bbuf[2 * q + 1], tbuf[2 * q + 1], NT)

    def alpha_part(window, pick):
        gap = 2 * window - 2 + pick - 5 * (pick // 2)
        level_only = (gap == 0) & (pick == 0) & (side == 0)
        wanted = ((gap > 0) & ((pick < 2) | (window >= 3))) | level_only

        @pl.when(wanted & (level + gap < depth))
        def _():
            across = pick // 2 + 1 - (gap + depth - 1) // depth
            add_alpha(chip_of(level + gap, side + across * (1 - 2 * side)))

    alpha_window = depth // 2 + 2

    def logit_copy(block):
        return remote(
            lsend.at[block], lrecv.at[chip], l_send.at[block], l_recv.at[chip], 2 * block + core
        )

    alpha_pass = remote(abuf.at[core], abuf.at[core], a_send, a_recv, partner)

    def before_alpha(block):
        gap = block // 2 - level
        across = lax.rem(lax.rem(block, 2) + side, 2)
        limit = alpha_window - 3 * across
        split = (across == 1) & is_split(block // 2)
        return (2 * gap <= limit) & (-2 * gap <= limit) & jnp.logical_not(split)

    def logit_part(block):
        part = dot(abuf[0], kbuf[block, 0], NT) + dot(abuf[1], kbuf[block, 1], NT)

        @pl.when(block != chip)
        def _():
            lsend[block] = part
            logit_copy(block).start()

        @pl.when(block == chip)
        def _():
            lrecv[block] = part

    def tile(block):
        def one(half):
            inner = dot(pbuf[block], cbuf[half], NT)
            value = inner * factor + 1.0
            kbuf[block, half] = (value * value * value).astype(jnp.bfloat16)

        each(2, one)

    def tile_item(window, sign):
        odd = lax.rem(window, 2)
        late = (window // (2 * depth)) * (1 - odd)
        across = odd + late
        gap = ((window - 3 * odd) // 2) * (1 - late) + late
        lev = level + sign * gap
        split = (across == 1) & is_split(lev)
        wanted = (gap >= 0) & ((gap > 0) | (sign < 0)) & inside(lev)
        wanted = wanted & (((late == 1) & split) | ((late == 0) & jnp.logical_not(split)))

        @pl.when(wanted)
        def _():
            block = chip_of(lev, side + across * (1 - 2 * side))

            @pl.when((across == 1) & (gap > 0))
            def _():
                each(PIECES, lambda piece: piece_wait(block, piece))

            tile(block)

            @pl.when(window > alpha_window)
            def _():
                logit_part(block)

    tri_copy(me).wait()
    asum[...] = dot(bbuf[me], tbuf[me], NT)
    beta_passed(chip)

    @pl.when(core == 0)
    def _():
        tri_copy(me + 1).wait()
        asum[...] += dot(bbuf[me + 1], tbuf[me + 1], NT)

    own_centres.wait()
    remote(centres, cbuf.at[1 - core], c_send, c_recv, partner).wait_recv()

    def forward(d, piece):
        @functools.partial(each, 2)
        def _(i):
            lev = level + (2 * i - 1) * d

            @pl.when(inside(lev))
            def _():
                piece_wait(chip_of(lev, side), piece)
                point_sends(lev, piece, lambda c: c.start())

        @pl.when(d == 1)
        def _():
            piece_wait(opposite, piece)
            relay_sends(piece, lambda c: c.start())

        @pl.when((d == depth - 2) & (piece == PIECES - 1))
        def _():
            each(PIECES, lambda late: split_sends(late, lambda c: c.start()))

    @functools.partial(each, 2 * depth + 2)
    def _(window):
        @functools.partial(each, depth)
        def _(lev):
            @pl.when((window == 0) & (lev > level))
            def _():
                beta_wait(chip_of(lev, side))
                beta_cross(lev).start()
                beta_pass(chip_of(lev, side)).start()

            @pl.when((window == 3) & (lev > level))
            def _():
                beta_arrive(chip_of(lev, 1 - side))

        @pl.when((window == 1) & (side == 0))
        def _():
            beta_arrive(opposite)

        @pl.when(window == alpha_window + 1)
        def _():
            remote(abuf.at[core], abuf.at[1 - core], a_send, a_recv, partner).wait_recv()

            @functools.partial(each, chips)
            def _(block):
                @pl.when(before_alpha(block))
                def _():
                    logit_part(block)

        each(2, lambda i: tile_item(window, 2 * i - 1))

        @pl.when(window <= alpha_window)
        def _():
            each(4, lambda pick: alpha_part(window, pick))

        @pl.when(window == alpha_window)
        def _():
            abuf[core] = asum[...].astype(jnp.bfloat16)
            alpha_pass.start()

        forward(window // PIECES + 1, lax.rem(window, PIECES))

    @functools.partial(each, chips)
    def _(q):
        @pl.when(q != chip)
        def _():
            remote(lsend.at[q], lrecv.at[q], l_send.at[q], l_recv.at[q], partner).wait_recv()

    logits = lrecv[0]
    for q in range(1, chips):
        logits = logits + lrecv[q]
    spot = lax.broadcasted_iota(jnp.int32, (classes, classes), 0)
    other = lax.broadcasted_iota(jnp.int32, (classes, classes), 1)
    row = jnp.broadcast_to(bias[...], (classes, classes))
    column = jnp.sum(jnp.where(spot == other, row, 0.0), axis=1, keepdims=True)
    logits = logits + column
    logits_out[...] = logits
    onehot = (labels[...] == lax.broadcasted_iota(jnp.int32, logits.shape, 0)).astype(jnp.float32)
    rbuf[chip] = (jax.nn.sigmoid(logits) - onehot).astype(jnp.bfloat16)

    def resid_copy(q):
        return remote(rbuf.at[chip], rbuf.at[chip], r_send.at[q], r_recv.at[chip], 2 * q + core)

    @functools.partial(each, chips)
    def _(q):
        @pl.when(q != chip)
        def _():
            resid_copy(q).start()

    mid = (depth + 1) // 2
    early = chips // 2

    def turn(i):
        pair = i // 2
        away = pair // 2
        lev = mid - 1 - away + lax.rem(pair, 2) * (2 * away + 1)
        return chip_of(lev, lax.rem(i, 2))

    def resid_wait(q):
        @pl.when(q != chip)
        def _():
            remote(rbuf.at[q], rbuf.at[q], r_send.at[q], r_recv.at[q], partner).wait_recv()

    gsend[...] = jnp.zeros_like(gsend)
    total[...] = jnp.zeros_like(total)

    @functools.partial(each, early)
    def _(i):
        q = turn(i)
        resid_wait(q)
        gsend[...] += dot(rbuf[q], kbuf[q, 1 - core], NN)
        total[...] += dot(rbuf[q], kbuf[q, core], NN)

    @functools.partial(each, chips - early)
    def _(i):
        q = turn(i + early)
        resid_wait(q)
        gsend[...] += dot(rbuf[q], kbuf[q, 1 - core], NN)

    grad_pass = remote(gsend, grecv, g_send, g_recv, partner)
    grad_pass.start()

    @functools.partial(each, chips - early)
    def _(i):
        q = turn(i + early)
        total[...] += dot(rbuf[q], kbuf[q, core], NN)

    mine = total[...]
    grad_pass.wait_recv()
    coeff = ((mine + grecv[...]) * (1.0 / math.sqrt(total_points))).astype(jnp.bfloat16)

    def term_copy(q):
        return remote(tsend.at[q], trecv.at[chip], ts_sem.at[q], tr_sem.at[chip], 2 * q + core)

    def pair_copy(q):
        return remote(xsend.at[q], xrecv.at[q], xs_sem.at[q], xr_sem.at[q], partner)

    def to_pair(q):
        return (q > chip) | ((q == chip) & (core == 0))

    def finish(q):
        pair_copy(q).wait_recv()
        tsend[q] = (xown[q] + xrecv[q]).astype(tsend.dtype)
        term_copy(q).start()

    @functools.partial(each, chips)
    def _(i):
        q = chips - 1 - i

        @pl.when(q > chip)
        def _():
            xsend[q] = dot(coeff, tbuf[2 * q + 1 - core], NN)
            xown[q] = dot(coeff, tbuf[2 * q + core], NN)
            pair_copy(q).start()

        @pl.when((q == chip) & (core == 0))
        def _():
            xsend[q] = dot(coeff, tbuf[2 * q + 1], NN)
            pair_copy(q).start()

        @pl.when(q == chip)
        def _():
            xown[q] = dot(coeff, tbuf[me], NN)

        @pl.when((q >= chip) & (q + 1 < chips))
        def _():
            finish(q + 1)

    total[...] = xown[chip]

    @pl.when(core == 1)
    def _():
        pair_copy(chip).wait_recv()
        total[...] += xrecv[chip]

    @functools.partial(each, chips)
    def _(q):
        @pl.when(q < chip)
        def _():
            remote(tsend.at[q], trecv.at[q], ts_sem.at[q], tr_sem.at[q], partner).wait_recv()
            total[...] += trecv[q].astype(jnp.float32)

    grad_out[...] = total[...]

    @functools.partial(each, chips)
    def _(q):
        @pl.when(beta_direct(q))
        def _():
            beta_send(q).wait_send()

        @pl.when(q > chip)
        def _():
            beta_pass(q).wait_send()

        @pl.when(q != chip)
        def _():
            logit_copy(q).wait_send()
            resid_copy(q).wait_send()

    @functools.partial(each, depth)
    def _(lev):
        @pl.when(lev > level)
        def _():
            beta_cross(lev).wait_send()

    own_pass.wait_send()
    centre_pass.wait_send()
    alpha_pass.wait_send()
    grad_pass.wait_send()
    @functools.partial(each, PIECES)
    def _(piece):
        each(depth, lambda lev: point_sends(lev, piece, lambda c: c.wait_send()))
        relay_sends(piece, lambda c: c.wait_send())
        split_sends(piece, lambda c: c.wait_send())


    @functools.partial(each, chips)
    def _(q):
        @pl.when(to_pair(q))
        def _():
            pair_copy(q).wait_send()

        @pl.when(q > chip)
        def _():
            term_copy(q).wait_send()


def write_out(grad, logits, grad_out, logits_out):
    grad_out[...] = grad[...]
    logits_out[...] = logits[...]


def on_device(points, labels, centres, tri_inverse, beta, bias):
    n = lax.axis_size("pts")
    chips = n // 2
    rows, features = points.shape
    size, classes = beta.shape
    low, full = jnp.bfloat16, jnp.float32
    dma = pltpu.SemaphoreType.DMA
    vmem = pl.BlockSpec(memory_space=pltpu.VMEM)
    hbm = pl.BlockSpec(memory_space=pl.ANY)
    grad_t, logits_t = pl.pallas_call(
        functools.partial(body, n),
        name="falkon_step",
        out_shape=(
            jax.ShapeDtypeStruct((classes, size), full),
            jax.ShapeDtypeStruct((classes, rows), full),
        ),
        in_specs=[hbm, vmem, hbm, hbm, vmem, vmem],
        out_specs=(vmem, vmem),
        scratch_shapes=[
            pltpu.VMEM((n, size, size), low),
            pltpu.VMEM((chips, rows, features), low),
            pltpu.VMEM((2, size, features), low),
            pltpu.VMEM((chips, 2, rows, size), low),
            pltpu.VMEM((n, classes, size), low),
            pltpu.VMEM((2, classes, size), low),
            pltpu.VMEM((classes, size), full),
            pltpu.VMEM((chips, classes, rows), full),
            pltpu.VMEM((chips, classes, rows), full),
            pltpu.VMEM((chips, classes, rows), low),
            pltpu.VMEM((classes, size), full),
            pltpu.VMEM((classes, size), full),
            pltpu.VMEM((chips, classes, size), low),
            pltpu.VMEM((chips, classes, size), low),
            pltpu.VMEM((classes, size), full),
            pltpu.VMEM((chips, classes, size), full),
            pltpu.VMEM((chips, classes, size), full),
            pltpu.VMEM((chips, classes, size), full),
            dma((n,)),
            dma((2,)),
            dma((chips,)),
            dma((n,)),
            dma((chips,)),
            dma((3, chips, PIECES)),
            dma((chips, PIECES)),
            dma, dma, dma, dma,
            dma((chips,)),
            dma((chips,)),
            dma((chips,)),
            dma((chips,)),
            dma, dma,
            dma((chips,)),
            dma((chips,)),
            dma((chips,)),
            dma((chips,)),
        ],
        compiler_params=pltpu.CompilerParams(
            collective_id=0, has_side_effects=True, vmem_limit_bytes=60 * 1024 * 1024
        ),
    )(points, labels[None, :], centres, tri_inverse, beta.T, bias[None, :])
    grad_t, logits_t = pl.pallas_call(
        write_out,
        name="write_out",
        out_shape=(
            jax.ShapeDtypeStruct(grad_t.shape, full),
            jax.ShapeDtypeStruct(logits_t.shape, full),
        ),
        in_specs=[vmem, vmem],
        out_specs=(vmem, vmem),
    )(grad_t, logits_t)
    return grad_t.T, logits_t.T


def solution(mesh):
    return jax.shard_map(
        on_device,
        mesh=mesh,
        in_specs=(
            P(("groups", "pts"), None),
            P(("groups", "pts")),
            P(("groups", "pts"), None),
            P(("groups", "pts"), None),
            P(("groups", "pts"), None),
            P("groups"),
        ),
        out_specs=(P(("groups", "pts"), None), P(("groups", "pts"), None)),
        check_vma=False,
    )
```

```python
import functools
import math

import jax
import jax.numpy as jnp
from jax import lax
from jax.experimental import pallas as pl
from jax.experimental.pallas import tpu as pltpu
from jax.sharding import PartitionSpec as P

NT = (((1,), (1,)), ((), ()))
NN = (((1,), (0,)), ((), ()))
PIECES = 2


def dot(left, right, dims):
    return lax.dot_general(left, right, dims, preferred_element_type=jnp.float32)


def body(
    n, points, labels, centres, tri, beta, bias, grad_out, logits_out,
    tbuf, pbuf, cbuf, kbuf, bbuf, abuf, asum, lsend, lrecv, rbuf, gsend, grecv, tsend, trecv, total, xsend, xrecv, xown,
    t_sem, own_sem, b_send, b_recv, f_send, p_send, p_recv, c_send, c_recv, a_send, a_recv,
    l_send, l_recv, r_send, r_recv, g_send, g_recv, ts_sem, tr_sem, xs_sem, xr_sem,
):
    chips = n // 2
    depth = chips // 2
    me = lax.axis_index("pts")
    core = lax.rem(me, 2)
    chip = me // 2
    side = lax.rem(chip, 2)
    level = chip // 2
    partner = me + 1 - 2 * core
    size = centres.shape[0]
    factor = 1.0 / math.sqrt(points.shape[1])
    total_points = n * points.shape[0]
    classes = beta.shape[0]

    def remote(src, dst, send, recv, target):
        return pltpu.make_async_remote_copy(
            src_ref=src, dst_ref=dst, send_sem=send, recv_sem=recv,
            device_id={"pts": target}, device_id_type=pl.DeviceIdType.MESH,
        )

    def tri_copy(j):
        start = pl.multiple_of(j * size, size)
        return pltpu.make_async_copy(tri.at[:, pl.ds(start, size)], tbuf.at[j], t_sem.at[j])

    def each(count, fn):
        lax.fori_loop(0, count, lambda i, c: (fn(i), c)[1], 0)

    own_points = pltpu.make_async_copy(points, pbuf.at[chip], own_sem.at[0])
    own_centres = pltpu.make_async_copy(centres, cbuf.at[core], own_sem.at[1])
    own_points.start()
    own_centres.start()

    @functools.partial(each, n)
    def _(j):
        @pl.when(j >= me)
        def _():
            tri_copy(j).start()

    barrier = pltpu.get_barrier_semaphore()

    @functools.partial(each, n)
    def _(q):
        @pl.when(q != me)
        def _():
            pl.semaphore_signal(
                barrier, inc=1, device_id={"pts": q}, device_id_type=pl.DeviceIdType.MESH
            )

    pl.semaphore_wait(barrier, n - 1)

    def beta_send(q):
        block = 2 * q + core
        return remote(beta, bbuf.at[me], b_send.at[q], b_recv.at[me], block)

    def beta_pass(q):
        block = 2 * q + core
        return remote(bbuf.at[block], bbuf.at[block], f_send.at[q], b_recv.at[block], partner)

    def beta_direct(q):
        return (q < chip) & ((lax.rem(q, 2) == side) | (q == chip - side))

    def beta_cross(lev):
        q = 2 * lev + side
        block = 2 * q + core
        target = 2 * (2 * level + 1 - side) + core
        return remote(bbuf.at[block], bbuf.at[block], b_send.at[q], b_recv.at[block], target)

    own_pass = remote(beta, bbuf.at[me], f_send.at[chip], b_recv.at[me], partner)
    centre_pass = remote(centres, cbuf.at[core], c_send, c_recv, partner)

    def chip_of(lev, sid):
        return 2 * lev + sid

    def inside(lev):
        return (lev >= 0) & (lev < depth)

    piece_rows = points.shape[0] // PIECES

    def point_copy(way, block, piece):
        target = (chip + 2, chip - 2, chip_of(level, 1 - side))[way]
        rows = pbuf.at[block, pl.ds(pl.multiple_of(piece * piece_rows, piece_rows), piece_rows)]
        return remote(
            rows, rows, p_send.at[way, block, piece], p_recv.at[block, piece], 2 * target + core
        )

    centre_pass.start()
    bbuf[me] = beta[...]
    relay = depth >= 4
    low_end, high_end = relay & (level == 0), relay & (level == depth - 1)
    near_low, near_high = relay & (level == 1), relay & (level == depth - 2)

    def is_split(lev):
        return (low_end & (lev == 1)) | (high_end & (lev == depth - 2))

    def crosses(lev, piece):
        relayed = (near_low & (lev == 0)) | (near_high & (lev == depth - 1))
        return jnp.logical_not(relayed | (is_split(lev) & (piece >= PIECES // 2)))

    def point_sends(lev, piece, act):
        block = chip_of(lev, side)
        for way, wanted in (
            (0, (lev <= level) & (level < depth - 1)),
            (1, (lev >= level) & (level > 0)),
            (2, crosses(lev, piece)),
        ):
            @pl.when(wanted)
            def _():
                act(point_copy(way, block, piece))

    opposite = chip_of(level, 1 - side)

    def relay_sends(piece, act):
        for way, end in ((0, low_end), (1, high_end)):
            @pl.when(end)
            def _():
                act(point_copy(way, opposite, piece))

    def split_sends(piece, act):
        for way, near in ((1, near_low), (0, near_high)):
            @pl.when(near & (piece >= PIECES // 2))
            def _():
                act(point_copy(way, opposite, piece))

    @functools.partial(each, chips)
    def _(i):
        q = chips - 1 - i

        @pl.when(beta_direct(q))
        def _():
            beta_send(q).start()

    own_pass.start()
    own_points.wait()
    each(PIECES, lambda piece: point_sends(level, piece, lambda c: c.start()))

    def piece_wait(block, piece):
        point_copy(2, block, piece).wait_recv()

    def beta_wait(q):
        block = 2 * q + core
        remote(beta, bbuf.at[block], b_send.at[0], b_recv.at[block], partner).wait_recv()

    def beta_arrive(q):
        beta_wait(q)
        beta_pass(q).start()

    def beta_passed(q):
        block = 2 * q + 1 - core
        remote(beta, bbuf.at[block], b_send.at[0], b_recv.at[block], partner).wait_recv()

    def add_alpha(q):
        beta_passed(q)
        tri_copy(2 * q).wait()
        tri_copy(2 * q + 1).wait()
        asum[...] += dot(bbuf[2 * q], tbuf[2 * q], NT) + dot(bbuf[2 * q + 1], tbuf[2 * q + 1], NT)

    def alpha_part(window, pick):
        second, odd = pick // 2, lax.rem(pick, 2)
        first = (1 - second) * (1 - odd)
        gap = first * (window + 1) + second * (2 * window - 6 + odd)
        level_only = (pick == 1) & (window == 1) & (side == 0)
        wanted = (gap > 0) & ((pick == 0) | ((pick > 1) & (window >= 3)))

        @pl.when((wanted | level_only) & (level + gap < depth))
        def _():
            add_alpha(chip_of(level + gap, side + (1 - first) * (1 - 2 * side)))

    alpha_window = max(depth - 2, (depth - 1) // 2 + 3)

    def logit_copy(block):
        return remote(
            lsend.at[block], lrecv.at[chip], l_send.at[block], l_recv.at[chip], 2 * block + core
        )

    alpha_pass = remote(abuf.at[core], abuf.at[core], a_send, a_recv, partner)

    def before_alpha(block):
        gap = block // 2 - level
        across = lax.rem(lax.rem(block, 2) + side, 2)
        limit = alpha_window - 3 * across
        split = (across == 1) & is_split(block // 2)
        return (2 * gap <= limit) & (-2 * gap <= limit) & jnp.logical_not(split)

    def logit_part(block):
        part = dot(abuf[0], kbuf[block, 0], NT) + dot(abuf[1], kbuf[block, 1], NT)

        @pl.when(block != chip)
        def _():
            lsend[block] = part
            logit_copy(block).start()

        @pl.when(block == chip)
        def _():
            lrecv[block] = part

    def tile(block):
        for half in range(2):
            inner = dot(pbuf[block], cbuf[half], NT)
            value = inner * factor + 1.0
            kbuf[block, half] = (value * value * value).astype(jnp.bfloat16)

    def tile_item(window, sign):
        odd = lax.rem(window, 2)
        late = (window // (2 * depth)) * (1 - odd)
        across = odd + late
        gap = ((window - 3 * odd) // 2) * (1 - late) + late
        lev = level + sign * gap
        split = (across == 1) & is_split(lev)
        wanted = (gap >= 0) & ((gap > 0) | (sign < 0)) & inside(lev)
        wanted = wanted & (((late == 1) & split) | ((late == 0) & jnp.logical_not(split)))

        @pl.when(wanted)
        def _():
            block = chip_of(lev, side + across * (1 - 2 * side))

            @pl.when((across == 1) & (gap > 0))
            def _():
                each(PIECES, lambda piece: piece_wait(block, piece))

            tile(block)

            @pl.when(window > alpha_window)
            def _():
                logit_part(block)

    tri_copy(me).wait()
    asum[...] = dot(bbuf[me], tbuf[me], NT)
    beta_passed(chip)

    @pl.when(core == 0)
    def _():
        tri_copy(me + 1).wait()
        asum[...] += dot(bbuf[me + 1], tbuf[me + 1], NT)

    own_centres.wait()
    remote(centres, cbuf.at[1 - core], c_send, c_recv, partner).wait_recv()

    def forward(d, piece):
        @functools.partial(each, 2)
        def _(i):
            lev = level + (2 * i - 1) * d

            @pl.when(inside(lev))
            def _():
                piece_wait(chip_of(lev, side), piece)
                point_sends(lev, piece, lambda c: c.start())

        @pl.when(d == 1)
        def _():
            piece_wait(opposite, piece)
            relay_sends(piece, lambda c: c.start())

        @pl.when((d == depth - 2) & (piece == PIECES - 1))
        def _():
            each(PIECES, lambda late: split_sends(late, lambda c: c.start()))

    @functools.partial(each, 2 * depth + 2)
    def _(window):
        @functools.partial(each, depth)
        def _(lev):
            @pl.when((window == 3) & (lev > level))
            def _():
                beta_arrive(chip_of(lev, 1 - side))

        @pl.when((window == 1) & (side == 0))
        def _():
            beta_arrive(opposite)

        @pl.when(window == alpha_window + 1)
        def _():
            remote(abuf.at[core], abuf.at[1 - core], a_send, a_recv, partner).wait_recv()

            @functools.partial(each, chips)
            def _(block):
                @pl.when(before_alpha(block))
                def _():
                    logit_part(block)

        each(2, lambda i: tile_item(window, 2 * i - 1))

        @functools.partial(each, depth)
        def _(lev):
            @pl.when((window == 0) & (lev > level))
            def _():
                beta_wait(chip_of(lev, side))
                beta_cross(lev).start()
                beta_pass(chip_of(lev, side)).start()


        @pl.when(window <= alpha_window)
        def _():
            each(4, lambda pick: alpha_part(window, pick))

        @pl.when(window == alpha_window)
        def _():
            abuf[core] = asum[...].astype(jnp.bfloat16)
            alpha_pass.start()

        forward(window // PIECES + 1, lax.rem(window, PIECES))

    @functools.partial(each, chips)
    def _(q):
        @pl.when(q != chip)
        def _():
            remote(lsend.at[q], lrecv.at[q], l_send.at[q], l_recv.at[q], partner).wait_recv()

    logits = lrecv[0]
    for q in range(1, chips):
        logits = logits + lrecv[q]
    spot = lax.broadcasted_iota(jnp.int32, (classes, classes), 0)
    other = lax.broadcasted_iota(jnp.int32, (classes, classes), 1)
    row = jnp.broadcast_to(bias[...], (classes, classes))
    column = jnp.sum(jnp.where(spot == other, row, 0.0), axis=1, keepdims=True)
    logits = logits + column
    logits_out[...] = logits
    onehot = (labels[...] == lax.broadcasted_iota(jnp.int32, logits.shape, 0)).astype(jnp.float32)
    rbuf[chip] = (jax.nn.sigmoid(logits) - onehot).astype(jnp.bfloat16)

    def resid_copy(q):
        return remote(rbuf.at[chip], rbuf.at[chip], r_send.at[q], r_recv.at[chip], 2 * q + core)

    @functools.partial(each, chips)
    def _(q):
        @pl.when(q != chip)
        def _():
            resid_copy(q).start()

    mid = (depth + 1) // 2
    early = chips // 2

    def turn(i):
        pair = i // 2
        away = pair // 2
        lev = mid - 1 - away + lax.rem(pair, 2) * (2 * away + 1)
        return chip_of(lev, lax.rem(i, 2))

    def resid_wait(q):
        @pl.when(q != chip)
        def _():
            remote(rbuf.at[q], rbuf.at[q], r_send.at[q], r_recv.at[q], partner).wait_recv()

    gsend[...] = jnp.zeros_like(gsend)
    total[...] = jnp.zeros_like(total)

    @functools.partial(each, early)
    def _(i):
        q = turn(i)
        resid_wait(q)
        gsend[...] += dot(rbuf[q], kbuf[q, 1 - core], NN)
        total[...] += dot(rbuf[q], kbuf[q, core], NN)

    @functools.partial(each, chips - early)
    def _(i):
        q = turn(i + early)
        resid_wait(q)
        gsend[...] += dot(rbuf[q], kbuf[q, 1 - core], NN)

    grad_pass = remote(gsend, grecv, g_send, g_recv, partner)
    grad_pass.start()

    @functools.partial(each, chips - early)
    def _(i):
        q = turn(i + early)
        total[...] += dot(rbuf[q], kbuf[q, core], NN)

    mine = total[...]
    grad_pass.wait_recv()
    coeff = ((mine + grecv[...]) * (1.0 / math.sqrt(total_points))).astype(jnp.bfloat16)

    def term_copy(q):
        return remote(tsend.at[q], trecv.at[chip], ts_sem.at[q], tr_sem.at[chip], 2 * q + core)

    def pair_copy(q):
        return remote(xsend.at[q], xrecv.at[q], xs_sem.at[q], xr_sem.at[q], partner)

    def to_pair(q):
        return (q > chip) | ((q == chip) & (core == 0))

    def finish(q):
        pair_copy(q).wait_recv()
        tsend[q] = (xown[q] + xrecv[q]).astype(tsend.dtype)
        term_copy(q).start()

    @functools.partial(each, chips)
    def _(i):
        q = chips - 1 - i

        @pl.when(q > chip)
        def _():
            xsend[q] = dot(coeff, tbuf[2 * q + 1 - core], NN)
            xown[q] = dot(coeff, tbuf[2 * q + core], NN)
            pair_copy(q).start()

        @pl.when((q == chip) & (core == 0))
        def _():
            xsend[q] = dot(coeff, tbuf[2 * q + 1], NN)
            pair_copy(q).start()

        @pl.when(q == chip)
        def _():
            xown[q] = dot(coeff, tbuf[me], NN)

        @pl.when((q >= chip) & (q + 1 < chips))
        def _():
            finish(q + 1)

    total[...] = xown[chip]

    @pl.when(core == 1)
    def _():
        pair_copy(chip).wait_recv()
        total[...] += xrecv[chip]

    @functools.partial(each, chips)
    def _(q):
        @pl.when(q < chip)
        def _():
            remote(tsend.at[q], trecv.at[q], ts_sem.at[q], tr_sem.at[q], partner).wait_recv()
            total[...] += trecv[q].astype(jnp.float32)

    grad_out[...] = total[...]

    @functools.partial(each, chips)
    def _(q):
        @pl.when(beta_direct(q))
        def _():
            beta_send(q).wait_send()

        @pl.when(q > chip)
        def _():
            beta_pass(q).wait_send()

        @pl.when(q != chip)
        def _():
            logit_copy(q).wait_send()
            resid_copy(q).wait_send()

    @functools.partial(each, depth)
    def _(lev):
        @pl.when(lev > level)
        def _():
            beta_cross(lev).wait_send()

    own_pass.wait_send()
    centre_pass.wait_send()
    alpha_pass.wait_send()
    grad_pass.wait_send()
    @functools.partial(each, PIECES)
    def _(piece):
        each(depth, lambda lev: point_sends(lev, piece, lambda c: c.wait_send()))
        relay_sends(piece, lambda c: c.wait_send())
        split_sends(piece, lambda c: c.wait_send())


    @functools.partial(each, chips)
    def _(q):
        @pl.when(to_pair(q))
        def _():
            pair_copy(q).wait_send()

        @pl.when(q > chip)
        def _():
            term_copy(q).wait_send()


def write_out(grad, logits, grad_out, logits_out):
    grad_out[...] = grad[...]
    logits_out[...] = logits[...]


def on_device(points, labels, centres, tri_inverse, beta, bias):
    n = lax.axis_size("pts")
    chips = n // 2
    rows, features = points.shape
    size, classes = beta.shape
    low, full = jnp.bfloat16, jnp.float32
    dma = pltpu.SemaphoreType.DMA
    vmem = pl.BlockSpec(memory_space=pltpu.VMEM)
    hbm = pl.BlockSpec(memory_space=pl.ANY)
    grad_t, logits_t = pl.pallas_call(
        functools.partial(body, n),
        name="falkon_step",
        out_shape=(
            jax.ShapeDtypeStruct((classes, size), full),
            jax.ShapeDtypeStruct((classes, rows), full),
        ),
        in_specs=[hbm, vmem, hbm, hbm, vmem, vmem],
        out_specs=(vmem, vmem),
        scratch_shapes=[
            pltpu.VMEM((n, size, size), low),
            pltpu.VMEM((chips, rows, features), low),
            pltpu.VMEM((2, size, features), low),
            pltpu.VMEM((chips, 2, rows, size), low),
            pltpu.VMEM((n, classes, size), low),
            pltpu.VMEM((2, classes, size), low),
            pltpu.VMEM((classes, size), full),
            pltpu.VMEM((chips, classes, rows), full),
            pltpu.VMEM((chips, classes, rows), full),
            pltpu.VMEM((chips, classes, rows), low),
            pltpu.VMEM((classes, size), full),
            pltpu.VMEM((classes, size), full),
            pltpu.VMEM((chips, classes, size), low),
            pltpu.VMEM((chips, classes, size), low),
            pltpu.VMEM((classes, size), full),
            pltpu.VMEM((chips, classes, size), full),
            pltpu.VMEM((chips, classes, size), full),
            pltpu.VMEM((chips, classes, size), full),
            dma((n,)),
            dma((2,)),
            dma((chips,)),
            dma((n,)),
            dma((chips,)),
            dma((3, chips, PIECES)),
            dma((chips, PIECES)),
            dma, dma, dma, dma,
            dma((chips,)),
            dma((chips,)),
            dma((chips,)),
            dma((chips,)),
            dma, dma,
            dma((chips,)),
            dma((chips,)),
            dma((chips,)),
            dma((chips,)),
        ],
        compiler_params=pltpu.CompilerParams(
            collective_id=0, has_side_effects=True, vmem_limit_bytes=60 * 1024 * 1024
        ),
    )(points, labels[None, :], centres, tri_inverse, beta.T, bias[None, :])
    grad_t, logits_t = pl.pallas_call(
        write_out,
        name="write_out",
        out_shape=(
            jax.ShapeDtypeStruct(grad_t.shape, full),
            jax.ShapeDtypeStruct(logits_t.shape, full),
        ),
        in_specs=[vmem, vmem],
        out_specs=(vmem, vmem),
    )(grad_t, logits_t)
    return grad_t.T, logits_t.T


def solution(mesh):
    return jax.shard_map(
        on_device,
        mesh=mesh,
        in_specs=(
            P(("groups", "pts"), None),
            P(("groups", "pts")),
            P(("groups", "pts"), None),
            P(("groups", "pts"), None),
            P(("groups", "pts"), None),
            P("groups"),
        ),
        out_specs=(P(("groups", "pts"), None), P(("groups", "pts"), None)),
        check_vma=False,
    )
```

```python
import functools
import math

import jax
import jax.numpy as jnp
from jax import lax
from jax.experimental import pallas as pl
from jax.experimental.pallas import tpu as pltpu
from jax.sharding import PartitionSpec as P

NT = (((1,), (1,)), ((), ()))
NN = (((1,), (0,)), ((), ()))
PIECES = 2


def dot(left, right, dims):
    return lax.dot_general(left, right, dims, preferred_element_type=jnp.float32)


def body(
    n, points, labels, centres, tri, beta, bias, grad_out, logits_out,
    tbuf, pbuf, cbuf, kbuf, bbuf, abuf, asum, lsend, lrecv, rbuf, gsend, grecv, tsend, trecv, total, xsend, xrecv, xown,
    t_sem, own_sem, b_send, b_recv, f_send, p_send, p_recv, c_send, c_recv, a_send, a_recv,
    l_send, l_recv, r_send, r_recv, g_send, g_recv, ts_sem, tr_sem, xs_sem, xr_sem,
):
    chips = n // 2
    depth = chips // 2
    me = lax.axis_index("pts")
    core = lax.rem(me, 2)
    chip = me // 2
    side = lax.rem(chip, 2)
    level = chip // 2
    partner = me + 1 - 2 * core
    size = centres.shape[0]
    factor = 1.0 / math.sqrt(points.shape[1])
    total_points = n * points.shape[0]
    classes = beta.shape[0]

    def remote(src, dst, send, recv, target):
        return pltpu.make_async_remote_copy(
            src_ref=src, dst_ref=dst, send_sem=send, recv_sem=recv,
            device_id={"pts": target}, device_id_type=pl.DeviceIdType.MESH,
        )

    def tri_copy(j):
        start = pl.multiple_of(j * size, size)
        return pltpu.make_async_copy(tri.at[:, pl.ds(start, size)], tbuf.at[j], t_sem.at[j])

    def each(count, fn):
        lax.fori_loop(0, count, lambda i, c: (fn(i), c)[1], 0)

    own_points = pltpu.make_async_copy(points, pbuf.at[chip], own_sem.at[0])
    own_centres = pltpu.make_async_copy(centres, cbuf.at[core], own_sem.at[1])
    own_points.start()
    own_centres.start()

    @functools.partial(each, n)
    def _(j):
        @pl.when(j >= me)
        def _():
            tri_copy(j).start()

    barrier = pltpu.get_barrier_semaphore()

    def greet(device):
        pl.semaphore_signal(
            barrier, inc=1, device_id={"pts": device}, device_id_type=pl.DeviceIdType.MESH
        )

    @functools.partial(each, depth)
    def _(lev):
        @pl.when((lev > level) | (lev == level - 1))
        def _():
            greet(2 * (2 * lev + side) + core)

    greet(2 * (2 * level + 1 - side) + core)
    greet(partner)
    above = 1 - level // (depth - 1) if depth > 1 else 0
    pl.semaphore_wait(barrier, level + above + 2)

    def beta_send(q):
        block = 2 * q + core
        return remote(beta, bbuf.at[me], b_send.at[q], b_recv.at[me], block)

    def beta_pass(q):
        block = 2 * q + core
        return remote(bbuf.at[block], bbuf.at[block], f_send.at[q], b_recv.at[block], partner)

    def beta_direct(q):
        return (q < chip) & ((lax.rem(q, 2) == side) | (q == chip - side))

    def beta_cross(lev):
        q = 2 * lev + side
        block = 2 * q + core
        target = 2 * (2 * level + 1 - side) + core
        return remote(bbuf.at[block], bbuf.at[block], b_send.at[q], b_recv.at[block], target)

    own_pass = remote(beta, bbuf.at[me], f_send.at[chip], b_recv.at[me], partner)
    centre_pass = remote(centres, cbuf.at[core], c_send, c_recv, partner)

    def chip_of(lev, sid):
        return 2 * lev + sid

    def inside(lev):
        return (lev >= 0) & (lev < depth)

    piece_rows = points.shape[0] // PIECES

    def point_copy(way, block, piece):
        target = (chip + 2, chip - 2, chip_of(level, 1 - side))[way]
        rows = pbuf.at[block, pl.ds(pl.multiple_of(piece * piece_rows, piece_rows), piece_rows)]
        return remote(
            rows, rows, p_send.at[way, block, piece], p_recv.at[block, piece], 2 * target + core
        )

    centre_pass.start()
    bbuf[me] = beta[...]
    relay = depth >= 4
    low_end, high_end = relay & (level == 0), relay & (level == depth - 1)
    near_low, near_high = relay & (level == 1), relay & (level == depth - 2)

    def is_split(lev):
        return (low_end & (lev == 1)) | (high_end & (lev == depth - 2))

    def crosses(lev, piece):
        relayed = (near_low & (lev == 0)) | (near_high & (lev == depth - 1))
        return jnp.logical_not(relayed | (is_split(lev) & (piece >= PIECES // 2)))

    def point_sends(lev, piece, act):
        block = chip_of(lev, side)
        for way, wanted in (
            (0, (lev <= level) & (level < depth - 1)),
            (1, (lev >= level) & (level > 0)),
            (2, crosses(lev, piece)),
        ):
            @pl.when(wanted)
            def _():
                act(point_copy(way, block, piece))

    opposite = chip_of(level, 1 - side)

    def relay_sends(piece, act):
        for way, end in ((0, low_end), (1, high_end)):
            @pl.when(end)
            def _():
                act(point_copy(way, opposite, piece))

    def split_sends(piece, act):
        for way, near in ((1, near_low), (0, near_high)):
            @pl.when(near & (piece >= PIECES // 2))
            def _():
                act(point_copy(way, opposite, piece))

    @functools.partial(each, chips)
    def _(i):
        q = chips - 1 - i

        @pl.when(beta_direct(q))
        def _():
            beta_send(q).start()

    own_pass.start()
    own_points.wait()
    each(PIECES, lambda piece: point_sends(level, piece, lambda c: c.start()))

    def piece_wait(block, piece):
        point_copy(2, block, piece).wait_recv()

    def beta_wait(q):
        block = 2 * q + core
        remote(beta, bbuf.at[block], b_send.at[0], b_recv.at[block], partner).wait_recv()

    def beta_arrive(q):
        beta_wait(q)
        beta_pass(q).start()

    def beta_passed(q):
        block = 2 * q + 1 - core
        remote(beta, bbuf.at[block], b_send.at[0], b_recv.at[block], partner).wait_recv()

    def add_alpha(q):
        beta_passed(q)
        tri_copy(2 * q).wait()
        tri_copy(2 * q + 1).wait()
        asum[...] += dot(bbuf[2 * q], tbuf[2 * q], NT) + dot(bbuf[2 * q + 1], tbuf[2 * q + 1], NT)

    def alpha_part(window, pick):
        second, odd = pick // 2, lax.rem(pick, 2)
        first = (1 - second) * (1 - odd)
        gap = first * (window + 1) + second * (2 * window - 6 + odd)
        level_only = (pick == 1) & (window == 1) & (side == 0)
        wanted = (gap > 0) & ((pick == 0) | ((pick > 1) & (window >= 3)))

        @pl.when((wanted | level_only) & (level + gap < depth))
        def _():
            add_alpha(chip_of(level + gap, side + (1 - first) * (1 - 2 * side)))

    alpha_window = max(depth - 2, (depth - 1) // 2 + 3)

    def logit_copy(block):
        return remote(
            lsend.at[block], lrecv.at[chip], l_send.at[block], l_recv.at[chip], 2 * block + core
        )

    alpha_pass = remote(abuf.at[core], abuf.at[core], a_send, a_recv, partner)

    def before_alpha(block):
        gap = block // 2 - level
        across = lax.rem(lax.rem(block, 2) + side, 2)
        limit = alpha_window - 3 * across
        split = (across == 1) & is_split(block // 2)
        return (2 * gap <= limit) & (-2 * gap <= limit) & jnp.logical_not(split)

    def logit_part(block):
        part = dot(abuf[0], kbuf[block, 0], NT) + dot(abuf[1], kbuf[block, 1], NT)

        @pl.when(block != chip)
        def _():
            lsend[block] = part
            logit_copy(block).start()

        @pl.when(block == chip)
        def _():
            lrecv[block] = part

    def tile(block):
        for half in range(2):
            inner = dot(pbuf[block], cbuf[half], NT)
            value = inner * factor + 1.0
            kbuf[block, half] = (value * value * value).astype(jnp.bfloat16)

    def tile_item(window, sign):
        odd = lax.rem(window, 2)
        late = (window // (2 * depth)) * (1 - odd)
        across = odd + late
        gap = ((window - 3 * odd) // 2) * (1 - late) + late
        lev = level + sign * gap
        split = (across == 1) & is_split(lev)
        wanted = (gap >= 0) & ((gap > 0) | (sign < 0)) & inside(lev)
        wanted = wanted & (((late == 1) & split) | ((late == 0) & jnp.logical_not(split)))

        @pl.when(wanted)
        def _():
            block = chip_of(lev, side + across * (1 - 2 * side))

            @pl.when((across == 1) & (gap > 0))
            def _():
                each(PIECES, lambda piece: piece_wait(block, piece))

            tile(block)

            @pl.when(window > alpha_window)
            def _():
                logit_part(block)

    tri_copy(me).wait()
    asum[...] = dot(bbuf[me], tbuf[me], NT)
    beta_passed(chip)

    @pl.when(core == 0)
    def _():
        tri_copy(me + 1).wait()
        asum[...] += dot(bbuf[me + 1], tbuf[me + 1], NT)

    own_centres.wait()
    remote(centres, cbuf.at[1 - core], c_send, c_recv, partner).wait_recv()

    def forward(d, piece):
        @functools.partial(each, 2)
        def _(i):
            lev = level + (2 * i - 1) * d

            @pl.when(inside(lev))
            def _():
                piece_wait(chip_of(lev, side), piece)
                point_sends(lev, piece, lambda c: c.start())

        @pl.when(d == 1)
        def _():
            piece_wait(opposite, piece)
            relay_sends(piece, lambda c: c.start())

        @pl.when((d == depth - 2) & (piece == PIECES - 1))
        def _():
            each(PIECES, lambda late: split_sends(late, lambda c: c.start()))

    @functools.partial(each, 2 * depth + 2)
    def _(window):
        @functools.partial(each, depth)
        def _(lev):
            @pl.when((window == 3) & (lev > level))
            def _():
                beta_arrive(chip_of(lev, 1 - side))

        @pl.when((window == 1) & (side == 0))
        def _():
            beta_arrive(opposite)

        @pl.when(window == alpha_window + 1)
        def _():
            remote(abuf.at[core], abuf.at[1 - core], a_send, a_recv, partner).wait_recv()

            @functools.partial(each, chips)
            def _(block):
                @pl.when(before_alpha(block))
                def _():
                    logit_part(block)

        each(2, lambda i: tile_item(window, 2 * i - 1))

        @functools.partial(each, depth)
        def _(lev):
            @pl.when((window == 0) & (lev > level))
            def _():
                beta_wait(chip_of(lev, side))
                beta_cross(lev).start()
                beta_pass(chip_of(lev, side)).start()


        @pl.when(window <= alpha_window)
        def _():
            each(4, lambda pick: alpha_part(window, pick))

        @pl.when(window == alpha_window)
        def _():
            abuf[core] = asum[...].astype(jnp.bfloat16)
            alpha_pass.start()

        forward(window // PIECES + 1, lax.rem(window, PIECES))

    @functools.partial(each, chips)
    def _(q):
        @pl.when(q != chip)
        def _():
            remote(lsend.at[q], lrecv.at[q], l_send.at[q], l_recv.at[q], partner).wait_recv()

    logits = lrecv[0]
    for q in range(1, chips):
        logits = logits + lrecv[q]
    spot = lax.broadcasted_iota(jnp.int32, (classes, classes), 0)
    other = lax.broadcasted_iota(jnp.int32, (classes, classes), 1)
    row = jnp.broadcast_to(bias[...], (classes, classes))
    column = jnp.sum(jnp.where(spot == other, row, 0.0), axis=1, keepdims=True)
    logits = logits + column
    logits_out[...] = logits
    onehot = (labels[...] == lax.broadcasted_iota(jnp.int32, logits.shape, 0)).astype(jnp.float32)
    rbuf[chip] = (jax.nn.sigmoid(logits) - onehot).astype(jnp.bfloat16)

    def resid_copy(q):
        return remote(rbuf.at[chip], rbuf.at[chip], r_send.at[q], r_recv.at[chip], 2 * q + core)

    @functools.partial(each, chips)
    def _(q):
        @pl.when(q != chip)
        def _():
            resid_copy(q).start()

    mid = (depth + 1) // 2
    early = chips // 2

    def turn(i):
        pair = i // 2
        away = pair // 2
        lev = mid - 1 - away + lax.rem(pair, 2) * (2 * away + 1)
        return chip_of(lev, lax.rem(i, 2))

    def resid_wait(q):
        @pl.when(q != chip)
        def _():
            remote(rbuf.at[q], rbuf.at[q], r_send.at[q], r_recv.at[q], partner).wait_recv()

    gsend[...] = jnp.zeros_like(gsend)
    total[...] = jnp.zeros_like(total)

    @functools.partial(each, early)
    def _(i):
        q = turn(i)
        resid_wait(q)
        gsend[...] += dot(rbuf[q], kbuf[q, 1 - core], NN)
        total[...] += dot(rbuf[q], kbuf[q, core], NN)

    @functools.partial(each, chips - early)
    def _(i):
        q = turn(i + early)
        resid_wait(q)
        gsend[...] += dot(rbuf[q], kbuf[q, 1 - core], NN)

    grad_pass = remote(gsend, grecv, g_send, g_recv, partner)
    grad_pass.start()

    @functools.partial(each, chips - early)
    def _(i):
        q = turn(i + early)
        total[...] += dot(rbuf[q], kbuf[q, core], NN)

    mine = total[...]
    grad_pass.wait_recv()
    coeff = ((mine + grecv[...]) * (1.0 / math.sqrt(total_points))).astype(jnp.bfloat16)

    def term_copy(q):
        return remote(tsend.at[q], trecv.at[chip], ts_sem.at[q], tr_sem.at[chip], 2 * q + core)

    def pair_copy(q):
        return remote(xsend.at[q], xrecv.at[q], xs_sem.at[q], xr_sem.at[q], partner)

    def to_pair(q):
        return (q > chip) | ((q == chip) & (core == 0))

    def finish(q):
        pair_copy(q).wait_recv()
        tsend[q] = (xown[q] + xrecv[q]).astype(tsend.dtype)
        term_copy(q).start()

    @functools.partial(each, chips)
    def _(i):
        q = chips - 1 - i

        @pl.when(q > chip)
        def _():
            xsend[q] = dot(coeff, tbuf[2 * q + 1 - core], NN)
            xown[q] = dot(coeff, tbuf[2 * q + core], NN)
            pair_copy(q).start()

        @pl.when((q == chip) & (core == 0))
        def _():
            xsend[q] = dot(coeff, tbuf[2 * q + 1], NN)
            pair_copy(q).start()

        @pl.when(q == chip)
        def _():
            xown[q] = dot(coeff, tbuf[me], NN)

        @pl.when((q >= chip) & (q + 1 < chips))
        def _():
            finish(q + 1)

    total[...] = xown[chip]

    @pl.when(core == 1)
    def _():
        pair_copy(chip).wait_recv()
        total[...] += xrecv[chip]

    @functools.partial(each, chips)
    def _(q):
        @pl.when(q < chip)
        def _():
            remote(tsend.at[q], trecv.at[q], ts_sem.at[q], tr_sem.at[q], partner).wait_recv()
            total[...] += trecv[q].astype(jnp.float32)

    grad_out[...] = total[...]

    @functools.partial(each, chips)
    def _(q):
        @pl.when(beta_direct(q))
        def _():
            beta_send(q).wait_send()

        @pl.when(q > chip)
        def _():
            beta_pass(q).wait_send()

        @pl.when(q != chip)
        def _():
            logit_copy(q).wait_send()
            resid_copy(q).wait_send()

    @functools.partial(each, depth)
    def _(lev):
        @pl.when(lev > level)
        def _():
            beta_cross(lev).wait_send()

    own_pass.wait_send()
    centre_pass.wait_send()
    alpha_pass.wait_send()
    grad_pass.wait_send()
    @functools.partial(each, PIECES)
    def _(piece):
        each(depth, lambda lev: point_sends(lev, piece, lambda c: c.wait_send()))
        relay_sends(piece, lambda c: c.wait_send())
        split_sends(piece, lambda c: c.wait_send())


    @functools.partial(each, chips)
    def _(q):
        @pl.when(to_pair(q))
        def _():
            pair_copy(q).wait_send()

        @pl.when(q > chip)
        def _():
            term_copy(q).wait_send()


def write_out(grad, logits, grad_out, logits_out):
    grad_out[...] = grad[...]
    logits_out[...] = logits[...]


def on_device(points, labels, centres, tri_inverse, beta, bias):
    n = lax.axis_size("pts")
    chips = n // 2
    rows, features = points.shape
    size, classes = beta.shape
    low, full = jnp.bfloat16, jnp.float32
    dma = pltpu.SemaphoreType.DMA
    vmem = pl.BlockSpec(memory_space=pltpu.VMEM)
    hbm = pl.BlockSpec(memory_space=pl.ANY)
    grad_t, logits_t = pl.pallas_call(
        functools.partial(body, n),
        name="falkon_step",
        out_shape=(
            jax.ShapeDtypeStruct((classes, size), full),
            jax.ShapeDtypeStruct((classes, rows), full),
        ),
        in_specs=[hbm, vmem, hbm, hbm, vmem, vmem],
        out_specs=(vmem, vmem),
        scratch_shapes=[
            pltpu.VMEM((n, size, size), low),
            pltpu.VMEM((chips, rows, features), low),
            pltpu.VMEM((2, size, features), low),
            pltpu.VMEM((chips, 2, rows, size), low),
            pltpu.VMEM((n, classes, size), low),
            pltpu.VMEM((2, classes, size), low),
            pltpu.VMEM((classes, size), full),
            pltpu.VMEM((chips, classes, rows), full),
            pltpu.VMEM((chips, classes, rows), full),
            pltpu.VMEM((chips, classes, rows), low),
            pltpu.VMEM((classes, size), full),
            pltpu.VMEM((classes, size), full),
            pltpu.VMEM((chips, classes, size), low),
            pltpu.VMEM((chips, classes, size), low),
            pltpu.VMEM((classes, size), full),
            pltpu.VMEM((chips, classes, size), full),
            pltpu.VMEM((chips, classes, size), full),
            pltpu.VMEM((chips, classes, size), full),
            dma((n,)),
            dma((2,)),
            dma((chips,)),
            dma((n,)),
            dma((chips,)),
            dma((3, chips, PIECES)),
            dma((chips, PIECES)),
            dma, dma, dma, dma,
            dma((chips,)),
            dma((chips,)),
            dma((chips,)),
            dma((chips,)),
            dma, dma,
            dma((chips,)),
            dma((chips,)),
            dma((chips,)),
            dma((chips,)),
        ],
        compiler_params=pltpu.CompilerParams(
            collective_id=0, has_side_effects=True, vmem_limit_bytes=60 * 1024 * 1024
        ),
    )(points, labels[None, :], centres, tri_inverse, beta.T, bias[None, :])
    grad_t, logits_t = pl.pallas_call(
        write_out,
        name="write_out",
        out_shape=(
            jax.ShapeDtypeStruct(grad_t.shape, full),
            jax.ShapeDtypeStruct(logits_t.shape, full),
        ),
        in_specs=[vmem, vmem],
        out_specs=(vmem, vmem),
    )(grad_t, logits_t)
    return grad_t.T, logits_t.T


def solution(mesh):
    return jax.shard_map(
        on_device,
        mesh=mesh,
        in_specs=(
            P(("groups", "pts"), None),
            P(("groups", "pts")),
            P(("groups", "pts"), None),
            P(("groups", "pts"), None),
            P(("groups", "pts"), None),
            P("groups"),
        ),
        out_specs=(P(("groups", "pts"), None), P(("groups", "pts"), None)),
        check_vma=False,
    )
```

```python
import functools
import math

import jax
import jax.numpy as jnp
from jax import lax
from jax.experimental import pallas as pl
from jax.experimental.pallas import tpu as pltpu
from jax.sharding import PartitionSpec as P

NT = (((1,), (1,)), ((), ()))
NN = (((1,), (0,)), ((), ()))
PIECES = 2


def dot(left, right, dims):
    return lax.dot_general(left, right, dims, preferred_element_type=jnp.float32)


def body(
    n, points, labels, centres, tri, beta, bias, grad_out, logits_out,
    tbuf, pbuf, cbuf, kbuf, bbuf, abuf, asum, lsend, lrecv, rbuf, gsend, grecv, tsend, trecv, total, xsend, xrecv, xown,
    t_sem, own_sem, b_send, b_recv, f_send, p_send, p_recv, c_send, c_recv, a_send, a_recv,
    l_send, l_recv, r_send, r_recv, g_send, g_recv, ts_sem, tr_sem, xs_sem, xr_sem,
):
    chips = n // 2
    depth = chips // 2
    me = lax.axis_index("pts")
    core = lax.rem(me, 2)
    chip = me // 2
    side = lax.rem(chip, 2)
    level = chip // 2
    partner = me + 1 - 2 * core
    size = centres.shape[0]
    factor = 1.0 / math.sqrt(points.shape[1])
    total_points = n * points.shape[0]
    classes = beta.shape[0]

    def remote(src, dst, send, recv, target):
        return pltpu.make_async_remote_copy(
            src_ref=src, dst_ref=dst, send_sem=send, recv_sem=recv,
            device_id={"pts": target}, device_id_type=pl.DeviceIdType.MESH,
        )

    def tri_copy(j):
        start = pl.multiple_of(j * size, size)
        return pltpu.make_async_copy(tri.at[:, pl.ds(start, size)], tbuf.at[j], t_sem.at[j])

    def each(count, fn):
        lax.fori_loop(0, count, lambda i, c: (fn(i), c)[1], 0)

    own_points = pltpu.make_async_copy(points, pbuf.at[chip], own_sem.at[0])
    own_centres = pltpu.make_async_copy(centres, cbuf.at[core], own_sem.at[1])
    own_points.start()
    own_centres.start()

    @functools.partial(each, n)
    def _(j):
        @pl.when(j >= me)
        def _():
            tri_copy(j).start()

    barrier = pltpu.get_barrier_semaphore()

    def greet(device):
        pl.semaphore_signal(
            barrier, inc=1, device_id={"pts": device}, device_id_type=pl.DeviceIdType.MESH
        )

    @functools.partial(each, depth)
    def _(lev):
        @pl.when((lev > level) | (lev == level - 1))
        def _():
            greet(2 * (2 * lev + side) + core)

    greet(2 * (2 * level + 1 - side) + core)
    greet(partner)
    above = 1 - level // (depth - 1) if depth > 1 else 0
    pl.semaphore_wait(barrier, level + above + 2)

    def beta_send(q):
        block = 2 * q + core
        return remote(beta, bbuf.at[me], b_send.at[q], b_recv.at[me], block)

    def beta_pass(q):
        block = 2 * q + core
        return remote(bbuf.at[block], bbuf.at[block], f_send.at[q], b_recv.at[block], partner)

    def beta_direct(q):
        return (q < chip) & ((lax.rem(q, 2) == side) | (q == chip - side))

    def beta_cross(lev):
        q = 2 * lev + side
        block = 2 * q + core
        target = 2 * (2 * level + 1 - side) + core
        return remote(bbuf.at[block], bbuf.at[block], b_send.at[q], b_recv.at[block], target)

    own_pass = remote(beta, bbuf.at[me], f_send.at[chip], b_recv.at[me], partner)
    centre_pass = remote(centres, cbuf.at[core], c_send, c_recv, partner)

    def chip_of(lev, sid):
        return 2 * lev + sid

    def inside(lev):
        return (lev >= 0) & (lev < depth)

    piece_rows = points.shape[0] // PIECES

    def point_copy(way, block, piece):
        target = (chip + 2, chip - 2, chip_of(level, 1 - side))[way]
        rows = pbuf.at[block, pl.ds(pl.multiple_of(piece * piece_rows, piece_rows), piece_rows)]
        return remote(
            rows, rows, p_send.at[way, block, piece], p_recv.at[block, piece], 2 * target + core
        )

    centre_pass.start()
    bbuf[me] = beta[...]
    relay = depth >= 4
    low_end, high_end = relay & (level == 0), relay & (level == depth - 1)
    near_low, near_high = relay & (level == 1), relay & (level == depth - 2)

    def is_split(lev):
        return (low_end & (lev == 1)) | (high_end & (lev == depth - 2))

    def crosses(lev, piece):
        relayed = (near_low & (lev == 0)) | (near_high & (lev == depth - 1))
        return jnp.logical_not(relayed | (is_split(lev) & (piece >= PIECES // 2)))

    def point_sends(lev, piece, act):
        block = chip_of(lev, side)
        for way, wanted in (
            (0, (lev <= level) & (level < depth - 1)),
            (1, (lev >= level) & (level > 0)),
            (2, crosses(lev, piece)),
        ):
            @pl.when(wanted)
            def _():
                act(point_copy(way, block, piece))

    opposite = chip_of(level, 1 - side)

    def relay_sends(piece, act):
        for way, end in ((0, low_end), (1, high_end)):
            @pl.when(end)
            def _():
                act(point_copy(way, opposite, piece))

    def split_sends(piece, act):
        for way, near in ((1, near_low), (0, near_high)):
            @pl.when(near & (piece >= PIECES // 2))
            def _():
                act(point_copy(way, opposite, piece))

    @functools.partial(each, chips)
    def _(i):
        q = chips - 1 - i

        @pl.when(beta_direct(q))
        def _():
            beta_send(q).start()

    own_pass.start()
    own_points.wait()
    each(PIECES, lambda piece: point_sends(level, piece, lambda c: c.start()))

    def piece_wait(block, piece):
        point_copy(2, block, piece).wait_recv()

    def beta_wait(q):
        block = 2 * q + core
        remote(beta, bbuf.at[block], b_send.at[0], b_recv.at[block], partner).wait_recv()

    def beta_arrive(q):
        beta_wait(q)
        beta_pass(q).start()

    def beta_passed(q):
        block = 2 * q + 1 - core
        remote(beta, bbuf.at[block], b_send.at[0], b_recv.at[block], partner).wait_recv()

    def add_alpha(q):
        beta_passed(q)
        tri_copy(2 * q).wait()
        tri_copy(2 * q + 1).wait()
        asum[...] += dot(bbuf[2 * q], tbuf[2 * q], NT) + dot(bbuf[2 * q + 1], tbuf[2 * q + 1], NT)

    def alpha_part(window, pick):
        second, odd = pick // 2, lax.rem(pick, 2)
        first = (1 - second) * (1 - odd)
        gap = first * (window + 1) + second * (2 * window - 6 + odd)
        level_only = (pick == 1) & (window == 1) & (side == 0)
        wanted = (gap > 0) & ((pick == 0) | ((pick > 1) & (window >= 3)))

        @pl.when((wanted | level_only) & (level + gap < depth))
        def _():
            add_alpha(chip_of(level + gap, side + (1 - first) * (1 - 2 * side)))

    alpha_window = max(depth - 2, (depth - 1) // 2 + 3)

    def logit_copy(block):
        return remote(
            lsend.at[block], lrecv.at[chip], l_send.at[block], l_recv.at[chip], 2 * block + core
        )

    alpha_pass = remote(abuf.at[core], abuf.at[core], a_send, a_recv, partner)

    def before_alpha(block):
        gap = block // 2 - level
        across = lax.rem(lax.rem(block, 2) + side, 2)
        limit = alpha_window + 1 - 3 * across
        split = (across == 1) & is_split(block // 2)
        return (2 * gap <= limit) & (-2 * gap <= limit) & jnp.logical_not(split)

    def logit_part(block):
        part = dot(abuf[0], kbuf[block, 0], NN) + dot(abuf[1], kbuf[block, 1], NN)

        @pl.when(block != chip)
        def _():
            lsend[block] = part
            logit_copy(block).start()

        @pl.when(block == chip)
        def _():
            lrecv[block] = part

    def tile(block):
        for half in range(2):
            inner = dot(cbuf[half], pbuf[block], NT)
            value = inner * factor + 1.0
            kbuf[block, half] = (value * value * value).astype(jnp.bfloat16)

    def tile_item(window, sign):
        odd = lax.rem(window, 2)
        late = (window // (2 * depth)) * (1 - odd)
        across = odd + late
        gap = ((window - 3 * odd) // 2) * (1 - late) + late
        lev = level + sign * gap
        split = (across == 1) & is_split(lev)
        wanted = (gap >= 0) & ((gap > 0) | (sign < 0)) & inside(lev)
        wanted = wanted & (((late == 1) & split) | ((late == 0) & jnp.logical_not(split)))

        @pl.when(wanted)
        def _():
            block = chip_of(lev, side + across * (1 - 2 * side))

            @pl.when((across == 1) & (gap > 0))
            def _():
                each(PIECES, lambda piece: piece_wait(block, piece))

            tile(block)

            @pl.when(window > alpha_window + 1)
            def _():
                logit_part(block)

    tri_copy(me).wait()
    asum[...] = dot(bbuf[me], tbuf[me], NT)
    beta_passed(chip)

    @pl.when(core == 0)
    def _():
        tri_copy(me + 1).wait()
        asum[...] += dot(bbuf[me + 1], tbuf[me + 1], NT)

    own_centres.wait()
    remote(centres, cbuf.at[1 - core], c_send, c_recv, partner).wait_recv()

    def forward(d, piece):
        @functools.partial(each, 2)
        def _(i):
            lev = level + (2 * i - 1) * d

            @pl.when(inside(lev))
            def _():
                piece_wait(chip_of(lev, side), piece)
                point_sends(lev, piece, lambda c: c.start())

        @pl.when(d == 1)
        def _():
            piece_wait(opposite, piece)
            relay_sends(piece, lambda c: c.start())

        @pl.when((d == depth - 2) & (piece == PIECES - 1))
        def _():
            each(PIECES, lambda late: split_sends(late, lambda c: c.start()))

    @functools.partial(each, 2 * depth + 2)
    def _(window):
        @functools.partial(each, depth)
        def _(lev):
            @pl.when((window == 3) & (lev > level))
            def _():
                beta_arrive(chip_of(lev, 1 - side))

        @pl.when((window == 1) & (side == 0))
        def _():
            beta_arrive(opposite)

        each(2, lambda i: tile_item(window, 2 * i - 1))

        @functools.partial(each, depth)
        def _(lev):
            @pl.when((window == 0) & (lev > level))
            def _():
                beta_wait(chip_of(lev, side))
                beta_cross(lev).start()
                beta_pass(chip_of(lev, side)).start()


        @pl.when(window <= alpha_window)
        def _():
            each(4, lambda pick: alpha_part(window, pick))

        @pl.when(window == alpha_window)
        def _():
            abuf[core] = asum[...].astype(jnp.bfloat16)
            alpha_pass.start()

        forward(window // PIECES + 1, lax.rem(window, PIECES))

        @pl.when(window == alpha_window + 1)
        def _():
            remote(abuf.at[core], abuf.at[1 - core], a_send, a_recv, partner).wait_recv()

            @functools.partial(each, chips)
            def _(block):
                @pl.when(before_alpha(block))
                def _():
                    logit_part(block)

    @functools.partial(each, chips)
    def _(q):
        @pl.when(q != chip)
        def _():
            remote(lsend.at[q], lrecv.at[q], l_send.at[q], l_recv.at[q], partner).wait_recv()

    logits = lrecv[0]
    for q in range(1, chips):
        logits = logits + lrecv[q]
    spot = lax.broadcasted_iota(jnp.int32, (classes, classes), 0)
    other = lax.broadcasted_iota(jnp.int32, (classes, classes), 1)
    row = jnp.broadcast_to(bias[...], (classes, classes))
    column = jnp.sum(jnp.where(spot == other, row, 0.0), axis=1, keepdims=True)
    logits = logits + column
    logits_out[...] = logits
    onehot = (labels[...] == lax.broadcasted_iota(jnp.int32, logits.shape, 0)).astype(jnp.float32)
    rbuf[chip] = (jax.nn.sigmoid(logits) - onehot).astype(jnp.bfloat16)

    def resid_copy(q):
        return remote(rbuf.at[chip], rbuf.at[chip], r_send.at[q], r_recv.at[chip], 2 * q + core)

    @functools.partial(each, chips)
    def _(q):
        @pl.when(q != chip)
        def _():
            resid_copy(q).start()

    mid = (depth + 1) // 2
    early = chips // 2

    def turn(i):
        pair = i // 2
        away = pair // 2
        lev = mid - 1 - away + lax.rem(pair, 2) * (2 * away + 1)
        return chip_of(lev, lax.rem(i, 2))

    def resid_wait(q):
        @pl.when(q != chip)
        def _():
            remote(rbuf.at[q], rbuf.at[q], r_send.at[q], r_recv.at[q], partner).wait_recv()

    gsend[...] = jnp.zeros_like(gsend)
    total[...] = jnp.zeros_like(total)

    @functools.partial(each, early)
    def _(i):
        q = turn(i)
        resid_wait(q)
        gsend[...] += dot(rbuf[q], kbuf[q, 1 - core], NT)
        total[...] += dot(rbuf[q], kbuf[q, core], NT)

    @functools.partial(each, chips - early)
    def _(i):
        q = turn(i + early)
        resid_wait(q)
        gsend[...] += dot(rbuf[q], kbuf[q, 1 - core], NT)

    grad_pass = remote(gsend, grecv, g_send, g_recv, partner)
    grad_pass.start()

    @functools.partial(each, chips - early)
    def _(i):
        q = turn(i + early)
        total[...] += dot(rbuf[q], kbuf[q, core], NT)

    mine = total[...]
    grad_pass.wait_recv()
    coeff = ((mine + grecv[...]) * (1.0 / math.sqrt(total_points))).astype(jnp.bfloat16)

    def term_copy(q):
        return remote(tsend.at[q], trecv.at[chip], ts_sem.at[q], tr_sem.at[chip], 2 * q + core)

    def pair_copy(q):
        return remote(xsend.at[q], xrecv.at[q], xs_sem.at[q], xr_sem.at[q], partner)

    def to_pair(q):
        return (q > chip) | ((q == chip) & (core == 0))

    def finish(q):
        pair_copy(q).wait_recv()
        tsend[q] = (xown[q] + xrecv[q]).astype(tsend.dtype)
        term_copy(q).start()

    @functools.partial(each, chips // 2)
    def _(i):
        q = chips - 1 - 2 * i

        @pl.when(q - 1 > chip)
        def _():
            xsend[q] = dot(coeff, tbuf[2 * q + 1 - core], NN)
            xsend[q - 1] = dot(coeff, tbuf[2 * q - 1 - core], NN)
            xown[q] = dot(coeff, tbuf[2 * q + core], NN)
            xown[q - 1] = dot(coeff, tbuf[2 * q - 2 + core], NN)
            pair_copy(q).start()
            pair_copy(q - 1).start()

        @pl.when(q - 1 == chip)
        def _():
            xsend[q] = dot(coeff, tbuf[2 * q + 1 - core], NN)
            xown[q] = dot(coeff, tbuf[2 * q + core], NN)
            pair_copy(q).start()

        @pl.when((q >= chip) & (q + 2 < chips))
        def _():
            finish(q + 2)
            finish(q + 1)

        own = q - 1 + lax.rem(chip, 2)

        @pl.when((own == chip) & (core == 0))
        def _():
            xsend[chip] = dot(coeff, tbuf[me + 1], NN)
            pair_copy(chip).start()

        @pl.when(own == chip)
        def _():
            xown[chip] = dot(coeff, tbuf[me], NN)

        @pl.when(q - 1 == chip)
        def _():
            finish(q)

    total[...] = xown[chip]

    @pl.when(core == 1)
    def _():
        pair_copy(chip).wait_recv()
        total[...] += xrecv[chip]

    @functools.partial(each, chips)
    def _(q):
        @pl.when(q < chip)
        def _():
            remote(tsend.at[q], trecv.at[q], ts_sem.at[q], tr_sem.at[q], partner).wait_recv()
            total[...] += trecv[q].astype(jnp.float32)

    grad_out[...] = total[...]

    @functools.partial(each, chips)
    def _(q):
        @pl.when(beta_direct(q))
        def _():
            beta_send(q).wait_send()

        @pl.when(q > chip)
        def _():
            beta_pass(q).wait_send()

        @pl.when(q != chip)
        def _():
            logit_copy(q).wait_send()
            resid_copy(q).wait_send()

    @functools.partial(each, depth)
    def _(lev):
        @pl.when(lev > level)
        def _():
            beta_cross(lev).wait_send()

    own_pass.wait_send()
    centre_pass.wait_send()
    alpha_pass.wait_send()
    grad_pass.wait_send()
    @functools.partial(each, PIECES)
    def _(piece):
        each(depth, lambda lev: point_sends(lev, piece, lambda c: c.wait_send()))
        relay_sends(piece, lambda c: c.wait_send())
        split_sends(piece, lambda c: c.wait_send())


    @functools.partial(each, chips)
    def _(q):
        @pl.when(to_pair(q))
        def _():
            pair_copy(q).wait_send()

        @pl.when(q > chip)
        def _():
            term_copy(q).wait_send()


def write_out(grad, logits, grad_out, logits_out):
    grad_out[...] = grad[...]
    logits_out[...] = logits[...]


def on_device(points, labels, centres, tri_inverse, beta, bias):
    n = lax.axis_size("pts")
    chips = n // 2
    rows, features = points.shape
    size, classes = beta.shape
    low, full = jnp.bfloat16, jnp.float32
    dma = pltpu.SemaphoreType.DMA
    vmem = pl.BlockSpec(memory_space=pltpu.VMEM)
    hbm = pl.BlockSpec(memory_space=pl.ANY)
    grad_t, logits_t = pl.pallas_call(
        functools.partial(body, n),
        name="falkon_step",
        out_shape=(
            jax.ShapeDtypeStruct((classes, size), full),
            jax.ShapeDtypeStruct((classes, rows), full),
        ),
        in_specs=[hbm, vmem, hbm, hbm, vmem, vmem],
        out_specs=(vmem, vmem),
        scratch_shapes=[
            pltpu.VMEM((n, size, size), low),
            pltpu.VMEM((chips, rows, features), low),
            pltpu.VMEM((2, size, features), low),
            pltpu.VMEM((chips, 2, size, rows), low),
            pltpu.VMEM((n, classes, size), low),
            pltpu.VMEM((2, classes, size), low),
            pltpu.VMEM((classes, size), full),
            pltpu.VMEM((chips, classes, rows), full),
            pltpu.VMEM((chips, classes, rows), full),
            pltpu.VMEM((chips, classes, rows), low),
            pltpu.VMEM((classes, size), full),
            pltpu.VMEM((classes, size), full),
            pltpu.VMEM((chips, classes, size), low),
            pltpu.VMEM((chips, classes, size), low),
            pltpu.VMEM((classes, size), full),
            pltpu.VMEM((chips, classes, size), full),
            pltpu.VMEM((chips, classes, size), full),
            pltpu.VMEM((chips, classes, size), full),
            dma((n,)),
            dma((2,)),
            dma((chips,)),
            dma((n,)),
            dma((chips,)),
            dma((3, chips, PIECES)),
            dma((chips, PIECES)),
            dma, dma, dma, dma,
            dma((chips,)),
            dma((chips,)),
            dma((chips,)),
            dma((chips,)),
            dma, dma,
            dma((chips,)),
            dma((chips,)),
            dma((chips,)),
            dma((chips,)),
        ],
        compiler_params=pltpu.CompilerParams(
            collective_id=0, has_side_effects=True, vmem_limit_bytes=60 * 1024 * 1024
        ),
    )(points, labels[None, :], centres, tri_inverse, beta.T, bias[None, :])
    grad_t, logits_t = pl.pallas_call(
        write_out,
        name="write_out",
        out_shape=(
            jax.ShapeDtypeStruct(grad_t.shape, full),
            jax.ShapeDtypeStruct(logits_t.shape, full),
        ),
        in_specs=[vmem, vmem],
        out_specs=(vmem, vmem),
    )(grad_t, logits_t)
    return grad_t.T, logits_t.T


def solution(mesh):
    return jax.shard_map(
        on_device,
        mesh=mesh,
        in_specs=(
            P(("groups", "pts"), None),
            P(("groups", "pts")),
            P(("groups", "pts"), None),
            P(("groups", "pts"), None),
            P(("groups", "pts"), None),
            P("groups"),
        ),
        out_specs=(P(("groups", "pts"), None), P(("groups", "pts"), None)),
        check_vma=False,
    )
```

```python
import functools
import math

import jax
import jax.numpy as jnp
from jax import lax
from jax.experimental import pallas as pl
from jax.experimental.pallas import tpu as pltpu
from jax.sharding import PartitionSpec as P

NT = (((1,), (1,)), ((), ()))
NN = (((1,), (0,)), ((), ()))
PIECES = 2


def dot(left, right, dims):
    return lax.dot_general(left, right, dims, preferred_element_type=jnp.float32)


def body(
    n, points, labels, centres, tri, beta, bias, grad_out, logits_out,
    tbuf, pbuf, cbuf, kbuf, bbuf, abuf, asum, lsend, lrecv, rbuf, gsend, grecv, tsend, trecv, total, xsend, xrecv, xown,
    t_sem, own_sem, b_send, b_recv, f_send, p_send, p_recv, c_send, c_recv, a_send, a_recv,
    l_send, l_recv, r_send, r_recv, g_send, g_recv, ts_sem, tr_sem, xs_sem, xr_sem,
):
    chips = n // 2
    depth = chips // 2
    me = lax.axis_index("pts")
    core = lax.rem(me, 2)
    chip = me // 2
    side = lax.rem(chip, 2)
    level = chip // 2
    partner = me + 1 - 2 * core
    size = centres.shape[0]
    factor = 1.0 / math.sqrt(points.shape[1])
    total_points = n * points.shape[0]
    classes = beta.shape[0]

    def remote(src, dst, send, recv, target):
        return pltpu.make_async_remote_copy(
            src_ref=src, dst_ref=dst, send_sem=send, recv_sem=recv,
            device_id={"pts": target}, device_id_type=pl.DeviceIdType.MESH,
        )

    def tri_copy(j):
        start = pl.multiple_of(j * size, size)
        return pltpu.make_async_copy(tri.at[:, pl.ds(start, size)], tbuf.at[j], t_sem.at[j])

    def each(count, fn):
        lax.fori_loop(0, count, lambda i, c: (fn(i), c)[1], 0)

    own_points = pltpu.make_async_copy(points, pbuf.at[chip], own_sem.at[0])
    own_centres = pltpu.make_async_copy(centres, cbuf.at[core], own_sem.at[1])
    own_points.start()
    own_centres.start()

    @functools.partial(each, n)
    def _(j):
        @pl.when(j >= me)
        def _():
            tri_copy(j).start()

    barrier = pltpu.get_barrier_semaphore()

    def greet(device):
        pl.semaphore_signal(
            barrier, inc=1, device_id={"pts": device}, device_id_type=pl.DeviceIdType.MESH
        )

    @functools.partial(each, depth)
    def _(lev):
        @pl.when((lev > level) | (lev == level - 1))
        def _():
            greet(2 * (2 * lev + side) + core)

    greet(2 * (2 * level + 1 - side) + core)
    greet(partner)
    above = 1 - level // (depth - 1) if depth > 1 else 0
    pl.semaphore_wait(barrier, level + above + 2)

    def beta_send(q):
        block = 2 * q + core
        return remote(beta, bbuf.at[me], b_send.at[q], b_recv.at[me], block)

    def beta_pass(q):
        block = 2 * q + core
        return remote(bbuf.at[block], bbuf.at[block], f_send.at[q], b_recv.at[block], partner)

    def beta_direct(q):
        return (q < chip) & ((lax.rem(q, 2) == side) | (q == chip - side))

    def beta_cross(lev):
        q = 2 * lev + side
        block = 2 * q + core
        target = 2 * (2 * level + 1 - side) + core
        return remote(bbuf.at[block], bbuf.at[block], b_send.at[q], b_recv.at[block], target)

    own_pass = remote(beta, bbuf.at[me], f_send.at[chip], b_recv.at[me], partner)
    centre_pass = remote(centres, cbuf.at[core], c_send, c_recv, partner)

    def chip_of(lev, sid):
        return 2 * lev + sid

    def inside(lev):
        return (lev >= 0) & (lev < depth)

    piece_rows = points.shape[0] // PIECES

    def point_copy(way, block, piece):
        target = (chip + 2, chip - 2, chip_of(level, 1 - side))[way]
        rows = pbuf.at[block, pl.ds(pl.multiple_of(piece * piece_rows, piece_rows), piece_rows)]
        return remote(
            rows, rows, p_send.at[way, block, piece], p_recv.at[block, piece], 2 * target + core
        )

    centre_pass.start()
    bbuf[me] = beta[...]
    relay = depth >= 4
    low_end, high_end = relay & (level == 0), relay & (level == depth - 1)
    near_low, near_high = relay & (level == 1), relay & (level == depth - 2)

    def is_split(lev):
        return (low_end & (lev == 1)) | (high_end & (lev == depth - 2))

    def crosses(lev, piece):
        relayed = (near_low & (lev == 0)) | (near_high & (lev == depth - 1))
        return jnp.logical_not(relayed | (is_split(lev) & (piece >= PIECES // 2)))

    def point_sends(lev, piece, act):
        block = chip_of(lev, side)
        for way, wanted in (
            (0, (lev <= level) & (level < depth - 1)),
            (1, (lev >= level) & (level > 0)),
            (2, crosses(lev, piece)),
        ):
            @pl.when(wanted)
            def _():
                act(point_copy(way, block, piece))

    opposite = chip_of(level, 1 - side)

    def relay_sends(piece, act):
        for way, end in ((0, low_end), (1, high_end)):
            @pl.when(end)
            def _():
                act(point_copy(way, opposite, piece))

    def split_sends(piece, act):
        for way, near in ((1, near_low), (0, near_high)):
            @pl.when(near & (piece >= PIECES // 2))
            def _():
                act(point_copy(way, opposite, piece))

    @functools.partial(each, chips)
    def _(i):
        q = chips - 1 - i

        @pl.when(beta_direct(q))
        def _():
            beta_send(q).start()

    own_pass.start()
    own_points.wait()
    each(PIECES, lambda piece: point_sends(level, piece, lambda c: c.start()))

    def piece_wait(block, piece):
        point_copy(2, block, piece).wait_recv()

    def beta_wait(q):
        block = 2 * q + core
        remote(beta, bbuf.at[block], b_send.at[0], b_recv.at[block], partner).wait_recv()

    def beta_arrive(q):
        beta_wait(q)
        beta_pass(q).start()

    def beta_passed(q):
        block = 2 * q + 1 - core
        remote(beta, bbuf.at[block], b_send.at[0], b_recv.at[block], partner).wait_recv()

    def add_alpha(q):
        beta_passed(q)
        tri_copy(2 * q).wait()
        tri_copy(2 * q + 1).wait()
        asum[...] += dot(bbuf[2 * q], tbuf[2 * q], NT) + dot(bbuf[2 * q + 1], tbuf[2 * q + 1], NT)

    def alpha_part(window, pick):
        second, odd = pick // 2, lax.rem(pick, 2)
        first = (1 - second) * (1 - odd)
        gap = first * (window + 1) + second * (2 * window - 6 + odd)
        level_only = (pick == 1) & (window == 1) & (side == 0)
        wanted = (gap > 0) & ((pick == 0) | ((pick > 1) & (window >= 3)))

        @pl.when((wanted | level_only) & (level + gap < depth))
        def _():
            add_alpha(chip_of(level + gap, side + (1 - first) * (1 - 2 * side)))

    alpha_window = max(depth - 2, (depth - 1) // 2 + 3)

    def logit_copy(block):
        return remote(
            lsend.at[block], lrecv.at[chip], l_send.at[block], l_recv.at[chip], 2 * block + core
        )

    alpha_pass = remote(abuf.at[core], abuf.at[core], a_send, a_recv, partner)

    def before_alpha(block):
        gap = block // 2 - level
        across = lax.rem(lax.rem(block, 2) + side, 2)
        limit = alpha_window + 1 - 3 * across
        split = (across == 1) & is_split(block // 2)
        return (2 * gap <= limit) & (-2 * gap <= limit) & jnp.logical_not(split)

    def logit_part(block):
        part = dot(abuf[0], kbuf[block, 0], NN) + dot(abuf[1], kbuf[block, 1], NN)

        @pl.when(block != chip)
        def _():
            lsend[block] = part
            logit_copy(block).start()

        @pl.when(block == chip)
        def _():
            lrecv[block] = part

    def tile(block):
        for half in range(2):
            inner = dot(cbuf[half], pbuf[block], NT)
            value = inner * factor + 1.0
            kbuf[block, half] = (value * value * value).astype(jnp.bfloat16)

    def tile_item(window, sign):
        odd = lax.rem(window, 2)
        late = (window // (2 * depth)) * (1 - odd)
        across = odd + late
        gap = ((window - 3 * odd) // 2) * (1 - late) + late
        lev = level + sign * gap
        split = (across == 1) & is_split(lev)
        wanted = (gap >= 0) & ((gap > 0) | (sign < 0)) & inside(lev)
        wanted = wanted & (((late == 1) & split) | ((late == 0) & jnp.logical_not(split)))

        @pl.when(wanted)
        def _():
            block = chip_of(lev, side + across * (1 - 2 * side))

            @pl.when((across == 1) & (gap > 0))
            def _():
                each(PIECES, lambda piece: piece_wait(block, piece))

            tile(block)

            @pl.when(window > alpha_window + 1)
            def _():
                logit_part(block)

    tri_copy(me).wait()
    asum[...] = dot(bbuf[me], tbuf[me], NT)
    beta_passed(chip)

    @pl.when(core == 0)
    def _():
        tri_copy(me + 1).wait()
        asum[...] += dot(bbuf[me + 1], tbuf[me + 1], NT)

    own_centres.wait()
    remote(centres, cbuf.at[1 - core], c_send, c_recv, partner).wait_recv()

    def forward(d, piece):
        @functools.partial(each, 2)
        def _(i):
            lev = level + (2 * i - 1) * d

            @pl.when(inside(lev))
            def _():
                piece_wait(chip_of(lev, side), piece)
                point_sends(lev, piece, lambda c: c.start())

        @pl.when(d == 1)
        def _():
            piece_wait(opposite, piece)
            relay_sends(piece, lambda c: c.start())

        @pl.when((d == depth - 2) & (piece == PIECES - 1))
        def _():
            each(PIECES, lambda late: split_sends(late, lambda c: c.start()))

    @functools.partial(each, 2 * depth + 2)
    def _(window):
        @functools.partial(each, depth)
        def _(lev):
            @pl.when((window == 3) & (lev > level))
            def _():
                beta_arrive(chip_of(lev, 1 - side))

        @pl.when((window == 1) & (side == 0))
        def _():
            beta_arrive(opposite)

        each(2, lambda i: tile_item(window, 2 * i - 1))

        @functools.partial(each, depth)
        def _(lev):
            @pl.when((window == 0) & (lev > level))
            def _():
                beta_wait(chip_of(lev, side))
                beta_cross(lev).start()
                beta_pass(chip_of(lev, side)).start()


        @pl.when(window <= alpha_window)
        def _():
            each(4, lambda pick: alpha_part(window, pick))

        @pl.when(window == alpha_window)
        def _():
            abuf[core] = asum[...].astype(jnp.bfloat16)
            alpha_pass.start()

        forward(window // PIECES + 1, lax.rem(window, PIECES))

        @pl.when(window == alpha_window + 1)
        def _():
            remote(abuf.at[core], abuf.at[1 - core], a_send, a_recv, partner).wait_recv()

            @functools.partial(each, chips)
            def _(block):
                @pl.when(before_alpha(block))
                def _():
                    logit_part(block)

    @functools.partial(each, chips)
    def _(q):
        @pl.when(q != chip)
        def _():
            remote(lsend.at[q], lrecv.at[q], l_send.at[q], l_recv.at[q], partner).wait_recv()

    logits = lrecv[0]
    for q in range(1, chips):
        logits = logits + lrecv[q]
    spot = lax.broadcasted_iota(jnp.int32, (classes, classes), 0)
    other = lax.broadcasted_iota(jnp.int32, (classes, classes), 1)
    row = jnp.broadcast_to(bias[...], (classes, classes))
    column = jnp.sum(jnp.where(spot == other, row, 0.0), axis=1, keepdims=True)
    logits = logits + column
    logits_out[...] = logits
    onehot = (labels[...] == lax.broadcasted_iota(jnp.int32, logits.shape, 0)).astype(jnp.float32)
    rbuf[chip] = (jax.nn.sigmoid(logits) - onehot).astype(jnp.bfloat16)

    def resid_copy(q):
        return remote(rbuf.at[chip], rbuf.at[chip], r_send.at[q], r_recv.at[chip], 2 * q + core)

    @functools.partial(each, chips)
    def _(q):
        @pl.when(q != chip)
        def _():
            resid_copy(q).start()

    mid = (depth + 1) // 2
    early = chips // 2

    def turn(i):
        pair = i // 2
        away = pair // 2
        lev = mid - 1 - away + lax.rem(pair, 2) * (2 * away + 1)
        return chip_of(lev, lax.rem(i, 2))

    def resid_wait(q):
        @pl.when(q != chip)
        def _():
            remote(rbuf.at[q], rbuf.at[q], r_send.at[q], r_recv.at[q], partner).wait_recv()

    gsend[...] = jnp.zeros_like(gsend)
    total[...] = jnp.zeros_like(total)

    @functools.partial(each, early)
    def _(i):
        q = turn(i)
        resid_wait(q)
        gsend[...] += dot(rbuf[q], kbuf[q, 1 - core], NT)
        total[...] += dot(rbuf[q], kbuf[q, core], NT)

    @functools.partial(each, chips - early)
    def _(i):
        q = turn(i + early)
        resid_wait(q)
        gsend[...] += dot(rbuf[q], kbuf[q, 1 - core], NT)

    grad_pass = remote(gsend, grecv, g_send, g_recv, partner)
    grad_pass.start()

    @functools.partial(each, chips - early)
    def _(i):
        q = turn(i + early)
        total[...] += dot(rbuf[q], kbuf[q, core], NT)

    mine = total[...]
    grad_pass.wait_recv()
    coeff = ((mine + grecv[...]) * (1.0 / math.sqrt(total_points))).astype(jnp.bfloat16)

    def term_copy(q):
        return remote(tsend.at[q], trecv.at[chip], ts_sem.at[q], tr_sem.at[chip], 2 * q + core)

    def pair_copy(q):
        return remote(xsend.at[q], xrecv.at[q], xs_sem.at[q], xr_sem.at[q], partner)

    def to_pair(q):
        return (q > chip) | ((q == chip) & (core == 0))

    def finish(q):
        pair_copy(q).wait_recv()
        tsend[q] = (xown[q] + xrecv[q]).astype(tsend.dtype)
        term_copy(q).start()

    @functools.partial(each, chips // 2)
    def _(i):
        q = chips - 1 - 2 * i

        @pl.when((q - 1 > chip) & (i == 0))
        def _():
            @functools.partial(each, 2)
            def _(k):
                xsend[q - k] = dot(coeff, tbuf[2 * (q - k) + 1 - core], NN)
                xown[q - k] = dot(coeff, tbuf[2 * (q - k) + core], NN)
                pair_copy(q - k).start()

            finish(q)

        @pl.when((q - 1 > chip) & (i > 0))
        def _():
            xsend[q] = dot(coeff, tbuf[2 * q + 1 - core], NN)
            xsend[q - 1] = dot(coeff, tbuf[2 * q - 1 - core], NN)
            xown[q] = dot(coeff, tbuf[2 * q + core], NN)
            xown[q - 1] = dot(coeff, tbuf[2 * q - 2 + core], NN)
            pair_copy(q).start()
            pair_copy(q - 1).start()

        @pl.when(q - 1 == chip)
        def _():
            xsend[q] = dot(coeff, tbuf[2 * q + 1 - core], NN)
            xown[q] = dot(coeff, tbuf[2 * q + core], NN)
            pair_copy(q).start()

        @pl.when((q >= chip) & (q + 2 < chips))
        def _():
            @pl.when(i > 1)
            def _():
                finish(q + 2)

            finish(q + 1)

        own = q - 1 + lax.rem(chip, 2)

        @pl.when((own == chip) & (core == 0))
        def _():
            xsend[chip] = dot(coeff, tbuf[me + 1], NN)
            pair_copy(chip).start()

        @pl.when(own == chip)
        def _():
            xown[chip] = dot(coeff, tbuf[me], NN)

        @pl.when(q - 1 == chip)
        def _():
            finish(q)

    total[...] = xown[chip]

    @pl.when(core == 1)
    def _():
        pair_copy(chip).wait_recv()
        total[...] += xrecv[chip]

    @functools.partial(each, chips)
    def _(q):
        @pl.when(q < chip)
        def _():
            remote(tsend.at[q], trecv.at[q], ts_sem.at[q], tr_sem.at[q], partner).wait_recv()
            total[...] += trecv[q].astype(jnp.float32)

    grad_out[...] = total[...]

    @functools.partial(each, chips)
    def _(q):
        @pl.when(beta_direct(q))
        def _():
            beta_send(q).wait_send()

        @pl.when(q > chip)
        def _():
            beta_pass(q).wait_send()

        @pl.when(q != chip)
        def _():
            logit_copy(q).wait_send()
            resid_copy(q).wait_send()

    @functools.partial(each, depth)
    def _(lev):
        @pl.when(lev > level)
        def _():
            beta_cross(lev).wait_send()

    own_pass.wait_send()
    centre_pass.wait_send()
    alpha_pass.wait_send()
    grad_pass.wait_send()
    @functools.partial(each, PIECES)
    def _(piece):
        each(depth, lambda lev: point_sends(lev, piece, lambda c: c.wait_send()))
        relay_sends(piece, lambda c: c.wait_send())
        split_sends(piece, lambda c: c.wait_send())


    @functools.partial(each, chips)
    def _(q):
        @pl.when(to_pair(q))
        def _():
            pair_copy(q).wait_send()

        @pl.when(q > chip)
        def _():
            term_copy(q).wait_send()


def write_out(grad, logits, grad_out, logits_out):
    grad_out[...] = grad[...]
    logits_out[...] = logits[...]


def on_device(points, labels, centres, tri_inverse, beta, bias):
    n = lax.axis_size("pts")
    chips = n // 2
    rows, features = points.shape
    size, classes = beta.shape
    low, full = jnp.bfloat16, jnp.float32
    dma = pltpu.SemaphoreType.DMA
    vmem = pl.BlockSpec(memory_space=pltpu.VMEM)
    hbm = pl.BlockSpec(memory_space=pl.ANY)
    grad_t, logits_t = pl.pallas_call(
        functools.partial(body, n),
        name="falkon_step",
        out_shape=(
            jax.ShapeDtypeStruct((classes, size), full),
            jax.ShapeDtypeStruct((classes, rows), full),
        ),
        in_specs=[hbm, vmem, hbm, hbm, vmem, vmem],
        out_specs=(vmem, vmem),
        scratch_shapes=[
            pltpu.VMEM((n, size, size), low),
            pltpu.VMEM((chips, rows, features), low),
            pltpu.VMEM((2, size, features), low),
            pltpu.VMEM((chips, 2, size, rows), low),
            pltpu.VMEM((n, classes, size), low),
            pltpu.VMEM((2, classes, size), low),
            pltpu.VMEM((classes, size), full),
            pltpu.VMEM((chips, classes, rows), full),
            pltpu.VMEM((chips, classes, rows), full),
            pltpu.VMEM((chips, classes, rows), low),
            pltpu.VMEM((classes, size), full),
            pltpu.VMEM((classes, size), full),
            pltpu.VMEM((chips, classes, size), low),
            pltpu.VMEM((chips, classes, size), low),
            pltpu.VMEM((classes, size), full),
            pltpu.VMEM((chips, classes, size), full),
            pltpu.VMEM((chips, classes, size), full),
            pltpu.VMEM((chips, classes, size), full),
            dma((n,)),
            dma((2,)),
            dma((chips,)),
            dma((n,)),
            dma((chips,)),
            dma((3, chips, PIECES)),
            dma((chips, PIECES)),
            dma, dma, dma, dma,
            dma((chips,)),
            dma((chips,)),
            dma((chips,)),
            dma((chips,)),
            dma, dma,
            dma((chips,)),
            dma((chips,)),
            dma((chips,)),
            dma((chips,)),
        ],
        compiler_params=pltpu.CompilerParams(
            collective_id=0, has_side_effects=True, vmem_limit_bytes=60 * 1024 * 1024
        ),
    )(points, labels[None, :], centres, tri_inverse, beta.T, bias[None, :])
    grad_t, logits_t = pl.pallas_call(
        write_out,
        name="write_out",
        out_shape=(
            jax.ShapeDtypeStruct(grad_t.shape, full),
            jax.ShapeDtypeStruct(logits_t.shape, full),
        ),
        in_specs=[vmem, vmem],
        out_specs=(vmem, vmem),
    )(grad_t, logits_t)
    return grad_t.T, logits_t.T


def solution(mesh):
    return jax.shard_map(
        on_device,
        mesh=mesh,
        in_specs=(
            P(("groups", "pts"), None),
            P(("groups", "pts")),
            P(("groups", "pts"), None),
            P(("groups", "pts"), None),
            P(("groups", "pts"), None),
            P("groups"),
        ),
        out_specs=(P(("groups", "pts"), None), P(("groups", "pts"), None)),
        check_vma=False,
    )
```

```python
import functools
import math

import jax
import jax.numpy as jnp
from jax import lax
from jax.experimental import pallas as pl
from jax.experimental.pallas import tpu as pltpu
from jax.sharding import PartitionSpec as P

NT = (((1,), (1,)), ((), ()))
NN = (((1,), (0,)), ((), ()))
PIECES = 2


def dot(left, right, dims):
    return lax.dot_general(left, right, dims, preferred_element_type=jnp.float32)


def body(
    n, points, labels, centres, tri, beta, bias, grad_out, logits_out,
    tbuf, pbuf, cbuf, kbuf, bbuf, abuf, asum, lsend, lrecv, rbuf, gsend, grecv, tsend, trecv, total, xsend, xrecv, xown,
    t_sem, own_sem, b_send, b_recv, f_send, p_send, p_recv, c_send, c_recv, a_send, a_recv,
    l_send, l_recv, r_send, r_recv, g_send, g_recv, ts_sem, tr_sem, xs_sem, xr_sem,
):
    chips = n // 2
    depth = chips // 2
    me = lax.axis_index("pts")
    core = lax.rem(me, 2)
    chip = me // 2
    side = lax.rem(chip, 2)
    level = chip // 2
    partner = me + 1 - 2 * core
    size = centres.shape[0]
    factor = 1.0 / math.sqrt(points.shape[1])
    total_points = n * points.shape[0]
    classes = beta.shape[0]

    def remote(src, dst, send, recv, target):
        return pltpu.make_async_remote_copy(
            src_ref=src, dst_ref=dst, send_sem=send, recv_sem=recv,
            device_id={"pts": target}, device_id_type=pl.DeviceIdType.MESH,
        )

    def tri_copy(j):
        start = pl.multiple_of(j * size, size)
        return pltpu.make_async_copy(tri.at[:, pl.ds(start, size)], tbuf.at[j], t_sem.at[j])

    def each(count, fn):
        lax.fori_loop(0, count, lambda i, c: (fn(i), c)[1], 0)

    own_points = pltpu.make_async_copy(points, pbuf.at[chip], own_sem.at[0])
    own_centres = pltpu.make_async_copy(centres, cbuf.at[core], own_sem.at[1])
    own_points.start()
    own_centres.start()

    @functools.partial(each, n)
    def _(j):
        @pl.when(j >= me)
        def _():
            tri_copy(j).start()

    barrier = pltpu.get_barrier_semaphore()

    def greet(device):
        pl.semaphore_signal(
            barrier, inc=1, device_id={"pts": device}, device_id_type=pl.DeviceIdType.MESH
        )

    @functools.partial(each, depth)
    def _(lev):
        @pl.when((lev > level) | (lev == level - 1))
        def _():
            greet(2 * (2 * lev + side) + core)

    greet(2 * (2 * level + 1 - side) + core)
    greet(partner)
    above = 1 - level // (depth - 1) if depth > 1 else 0
    pl.semaphore_wait(barrier, level + above + 2)

    def beta_send(q):
        block = 2 * q + core
        return remote(beta, bbuf.at[me], b_send.at[q], b_recv.at[me], block)

    def beta_pass(q):
        block = 2 * q + core
        return remote(bbuf.at[block], bbuf.at[block], f_send.at[q], b_recv.at[block], partner)

    def beta_direct(q):
        return (q < chip) & ((lax.rem(q, 2) == side) | (q == chip - side))

    def beta_cross(lev):
        q = 2 * lev + side
        block = 2 * q + core
        target = 2 * (2 * level + 1 - side) + core
        return remote(bbuf.at[block], bbuf.at[block], b_send.at[q], b_recv.at[block], target)

    own_pass = remote(beta, bbuf.at[me], f_send.at[chip], b_recv.at[me], partner)
    centre_pass = remote(centres, cbuf.at[core], c_send, c_recv, partner)

    def chip_of(lev, sid):
        return 2 * lev + sid

    def inside(lev):
        return (lev >= 0) & (lev < depth)

    piece_rows = points.shape[0] // PIECES

    def point_copy(way, block, piece):
        target = (chip + 2, chip - 2, chip_of(level, 1 - side))[way]
        rows = pbuf.at[block, pl.ds(pl.multiple_of(piece * piece_rows, piece_rows), piece_rows)]
        return remote(
            rows, rows, p_send.at[way, block, piece], p_recv.at[block, piece], 2 * target + core
        )

    centre_pass.start()
    bbuf[me] = beta[...]
    relay = depth >= 4
    low_end, high_end = relay & (level == 0), relay & (level == depth - 1)
    near_low, near_high = relay & (level == 1), relay & (level == depth - 2)

    def is_split(lev):
        return (low_end & (lev == 1)) | (high_end & (lev == depth - 2))

    def crosses(lev, piece):
        relayed = (near_low & (lev == 0)) | (near_high & (lev == depth - 1))
        return jnp.logical_not(relayed | (is_split(lev) & (piece >= PIECES // 2)))

    def point_sends(lev, piece, act):
        block = chip_of(lev, side)
        for way, wanted in (
            (0, (lev <= level) & (level < depth - 1)),
            (1, (lev >= level) & (level > 0)),
            (2, crosses(lev, piece)),
        ):
            @pl.when(wanted)
            def _():
                act(point_copy(way, block, piece))

    opposite = chip_of(level, 1 - side)

    def relay_sends(piece, act):
        for way, end in ((0, low_end), (1, high_end)):
            @pl.when(end)
            def _():
                act(point_copy(way, opposite, piece))

    def split_sends(piece, act):
        for way, near in ((1, near_low), (0, near_high)):
            @pl.when(near & (piece >= PIECES // 2))
            def _():
                act(point_copy(way, opposite, piece))

    @functools.partial(each, chips)
    def _(i):
        q = chips - 1 - i

        @pl.when(beta_direct(q))
        def _():
            beta_send(q).start()

    own_pass.start()
    own_points.wait()
    each(PIECES, lambda piece: point_sends(level, piece, lambda c: c.start()))

    def piece_wait(block, piece):
        point_copy(2, block, piece).wait_recv()

    def beta_wait(q):
        block = 2 * q + core
        remote(beta, bbuf.at[block], b_send.at[0], b_recv.at[block], partner).wait_recv()

    def beta_arrive(q):
        beta_wait(q)
        beta_pass(q).start()

    def beta_passed(q):
        block = 2 * q + 1 - core
        remote(beta, bbuf.at[block], b_send.at[0], b_recv.at[block], partner).wait_recv()

    def add_alpha(q):
        beta_passed(q)
        tri_copy(2 * q).wait()
        tri_copy(2 * q + 1).wait()
        asum[...] += dot(bbuf[2 * q], tbuf[2 * q], NT) + dot(bbuf[2 * q + 1], tbuf[2 * q + 1], NT)

    def alpha_part(window, pick):
        second, odd = pick // 2, lax.rem(pick, 2)
        first = (1 - second) * (1 - odd)
        gap = first * (window + 1) + second * (2 * window - 6 + odd)
        level_only = (pick == 1) & (window == 1) & (side == 0)
        wanted = (gap > 0) & ((pick == 0) | ((pick > 1) & (window >= 3)))

        @pl.when((wanted | level_only) & (level + gap < depth))
        def _():
            add_alpha(chip_of(level + gap, side + (1 - first) * (1 - 2 * side)))

    alpha_window = max(depth - 2, (depth - 1) // 2 + 3)

    def logit_copy(block):
        return remote(
            lsend.at[block], lrecv.at[chip], l_send.at[block], l_recv.at[chip], 2 * block + core
        )

    alpha_pass = remote(abuf.at[core], abuf.at[core], a_send, a_recv, partner)

    def before_alpha(block):
        gap = block // 2 - level
        across = lax.rem(lax.rem(block, 2) + side, 2)
        limit = alpha_window + 1 - 3 * across
        split = (across == 1) & is_split(block // 2)
        return (2 * gap <= limit) & (-2 * gap <= limit) & jnp.logical_not(split)

    def logit_part(block):
        part = dot(abuf[0], kbuf[block, 0], NN) + dot(abuf[1], kbuf[block, 1], NN)

        @pl.when(block != chip)
        def _():
            lsend[block] = part
            logit_copy(block).start()

        @pl.when(block == chip)
        def _():
            lrecv[block] = part

    def tile(block):
        for half in range(2):
            inner = dot(cbuf[half], pbuf[block], NT)
            value = inner * factor + 1.0
            kbuf[block, half] = (value * value * value).astype(jnp.bfloat16)

    def tile_item(window, sign):
        odd = lax.rem(window, 2)
        late = (window // (2 * depth)) * (1 - odd)
        across = odd + late
        gap = ((window - 3 * odd) // 2) * (1 - late) + late
        lev = level + sign * gap
        split = (across == 1) & is_split(lev)
        wanted = (gap >= 0) & ((gap > 0) | (sign < 0)) & inside(lev)
        wanted = wanted & (((late == 1) & split) | ((late == 0) & jnp.logical_not(split)))

        @pl.when(wanted)
        def _():
            block = chip_of(lev, side + across * (1 - 2 * side))

            @pl.when((across == 1) & (gap > 0))
            def _():
                each(PIECES, lambda piece: piece_wait(block, piece))

            tile(block)

            @pl.when(window > alpha_window + 1)
            def _():
                logit_part(block)

    tri_copy(me).wait()
    asum[...] = dot(bbuf[me], tbuf[me], NT)
    beta_passed(chip)

    @pl.when(core == 0)
    def _():
        tri_copy(me + 1).wait()
        asum[...] += dot(bbuf[me + 1], tbuf[me + 1], NT)

    own_centres.wait()
    remote(centres, cbuf.at[1 - core], c_send, c_recv, partner).wait_recv()

    def forward(d, piece):
        @functools.partial(each, 2)
        def _(i):
            lev = level + (2 * i - 1) * d

            @pl.when(inside(lev))
            def _():
                piece_wait(chip_of(lev, side), piece)
                point_sends(lev, piece, lambda c: c.start())

        @pl.when(d == 1)
        def _():
            piece_wait(opposite, piece)
            relay_sends(piece, lambda c: c.start())

        @pl.when((d == depth - 2) & (piece == PIECES - 1))
        def _():
            each(PIECES, lambda late: split_sends(late, lambda c: c.start()))

    @functools.partial(each, 2 * depth + 2)
    def _(window):
        @functools.partial(each, depth)
        def _(lev):
            @pl.when((window == 3) & (lev > level))
            def _():
                beta_arrive(chip_of(lev, 1 - side))

        @pl.when((window == 1) & (side == 0))
        def _():
            beta_arrive(opposite)

        each(2, lambda i: tile_item(window, 2 * i - 1))

        @functools.partial(each, depth)
        def _(lev):
            @pl.when((window == 0) & (lev > level))
            def _():
                beta_wait(chip_of(lev, side))
                beta_cross(lev).start()
                beta_pass(chip_of(lev, side)).start()


        @pl.when(window <= alpha_window)
        def _():
            each(4, lambda pick: alpha_part(window, pick))

        @pl.when(window == alpha_window)
        def _():
            abuf[core] = asum[...].astype(jnp.bfloat16)
            alpha_pass.start()

        forward(window // PIECES + 1, lax.rem(window, PIECES))

        @pl.when(window == alpha_window + 1)
        def _():
            remote(abuf.at[core], abuf.at[1 - core], a_send, a_recv, partner).wait_recv()

            @functools.partial(each, chips)
            def _(block):
                @pl.when(before_alpha(block))
                def _():
                    logit_part(block)

    spot = lax.broadcasted_iota(jnp.int32, (classes, classes), 0)
    other = lax.broadcasted_iota(jnp.int32, (classes, classes), 1)
    row = jnp.broadcast_to(bias[...], (classes, classes))
    column = jnp.sum(jnp.where(spot == other, row, 0.0), axis=1, keepdims=True)
    gsend[...] = jnp.zeros_like(gsend)
    total[...] = jnp.zeros_like(total)

    def add_logits(q, acc):
        @pl.when(q != chip)
        def _():
            remote(lsend.at[q], lrecv.at[q], l_send.at[q], l_recv.at[q], partner).wait_recv()

        return acc + lrecv[q]

    logits = lax.fori_loop(0, chips, add_logits, jnp.zeros(lrecv.shape[1:], jnp.float32)) + column
    logits_out[...] = logits
    onehot = (labels[...] == lax.broadcasted_iota(jnp.int32, logits.shape, 0)).astype(jnp.float32)
    rbuf[chip] = (jax.nn.sigmoid(logits) - onehot).astype(jnp.bfloat16)

    def resid_copy(q):
        return remote(rbuf.at[chip], rbuf.at[chip], r_send.at[q], r_recv.at[chip], 2 * q + core)

    @functools.partial(each, chips)
    def _(q):
        @pl.when(q != chip)
        def _():
            resid_copy(q).start()

    mid = (depth + 1) // 2
    early = chips // 2

    def turn(i):
        pair = i // 2
        away = pair // 2
        lev = mid - 1 - away + lax.rem(pair, 2) * (2 * away + 1)
        return chip_of(lev, lax.rem(i, 2))

    def resid_wait(q):
        @pl.when(q != chip)
        def _():
            remote(rbuf.at[q], rbuf.at[q], r_send.at[q], r_recv.at[q], partner).wait_recv()

    @functools.partial(each, early)
    def _(i):
        q = turn(i)
        resid_wait(q)
        gsend[...] += dot(rbuf[q], kbuf[q, 1 - core], NT)
        total[...] += dot(rbuf[q], kbuf[q, core], NT)

    @functools.partial(each, chips - early)
    def _(i):
        q = turn(i + early)
        resid_wait(q)
        gsend[...] += dot(rbuf[q], kbuf[q, 1 - core], NT)

    grad_pass = remote(gsend, grecv, g_send, g_recv, partner)
    grad_pass.start()

    @functools.partial(each, chips - early)
    def _(i):
        q = turn(i + early)
        total[...] += dot(rbuf[q], kbuf[q, core], NT)

    mine = total[...]
    grad_pass.wait_recv()
    coeff = ((mine + grecv[...]) * (1.0 / math.sqrt(total_points))).astype(jnp.bfloat16)

    def term_copy(q):
        return remote(tsend.at[q], trecv.at[chip], ts_sem.at[q], tr_sem.at[chip], 2 * q + core)

    def pair_copy(q):
        return remote(xsend.at[q], xrecv.at[q], xs_sem.at[q], xr_sem.at[q], partner)

    def to_pair(q):
        return (q > chip) | ((q == chip) & (core == 0))

    def finish(q):
        pair_copy(q).wait_recv()
        tsend[q] = (xown[q] + xrecv[q]).astype(tsend.dtype)
        term_copy(q).start()

    @functools.partial(each, chips // 2)
    def _(i):
        q = chips - 1 - 2 * i

        @pl.when((q - 1 > chip) & (i == 0))
        def _():
            @functools.partial(each, 2)
            def _(k):
                xsend[q - k] = dot(coeff, tbuf[2 * (q - k) + 1 - core], NN)
                xown[q - k] = dot(coeff, tbuf[2 * (q - k) + core], NN)
                pair_copy(q - k).start()

            finish(q)

        @pl.when((q - 1 > chip) & (i > 0))
        def _():
            xsend[q] = dot(coeff, tbuf[2 * q + 1 - core], NN)
            xsend[q - 1] = dot(coeff, tbuf[2 * q - 1 - core], NN)
            xown[q] = dot(coeff, tbuf[2 * q + core], NN)
            xown[q - 1] = dot(coeff, tbuf[2 * q - 2 + core], NN)
            pair_copy(q).start()
            pair_copy(q - 1).start()

        @pl.when(q - 1 == chip)
        def _():
            xsend[q] = dot(coeff, tbuf[2 * q + 1 - core], NN)
            xown[q] = dot(coeff, tbuf[2 * q + core], NN)
            pair_copy(q).start()

        @pl.when((q >= chip) & (q + 2 < chips))
        def _():
            @pl.when(i > 1)
            def _():
                finish(q + 2)

            finish(q + 1)

        own = q - 1 + lax.rem(chip, 2)

        @pl.when((own == chip) & (core == 0))
        def _():
            xsend[chip] = dot(coeff, tbuf[me + 1], NN)
            pair_copy(chip).start()

        @pl.when(own == chip)
        def _():
            xown[chip] = dot(coeff, tbuf[me], NN)

        @pl.when(q - 1 == chip)
        def _():
            finish(q)

    total[...] = xown[chip]

    @pl.when(core == 1)
    def _():
        pair_copy(chip).wait_recv()
        total[...] += xrecv[chip]

    @functools.partial(each, chips)
    def _(q):
        @pl.when(q < chip)
        def _():
            remote(tsend.at[q], trecv.at[q], ts_sem.at[q], tr_sem.at[q], partner).wait_recv()
            total[...] += trecv[q].astype(jnp.float32)

    grad_out[...] = total[...]

    @functools.partial(each, chips)
    def _(q):
        @pl.when(beta_direct(q))
        def _():
            beta_send(q).wait_send()

        @pl.when(q > chip)
        def _():
            beta_pass(q).wait_send()

        @pl.when(q != chip)
        def _():
            logit_copy(q).wait_send()
            resid_copy(q).wait_send()

    @functools.partial(each, depth)
    def _(lev):
        @pl.when(lev > level)
        def _():
            beta_cross(lev).wait_send()

    own_pass.wait_send()
    centre_pass.wait_send()
    alpha_pass.wait_send()
    grad_pass.wait_send()
    @functools.partial(each, PIECES)
    def _(piece):
        each(depth, lambda lev: point_sends(lev, piece, lambda c: c.wait_send()))
        relay_sends(piece, lambda c: c.wait_send())
        split_sends(piece, lambda c: c.wait_send())


    @functools.partial(each, chips)
    def _(q):
        @pl.when(to_pair(q))
        def _():
            pair_copy(q).wait_send()

        @pl.when(q > chip)
        def _():
            term_copy(q).wait_send()


def write_out(grad, logits, grad_out, logits_out):
    grad_out[...] = grad[...]
    logits_out[...] = logits[...]


def on_device(points, labels, centres, tri_inverse, beta, bias):
    n = lax.axis_size("pts")
    chips = n // 2
    rows, features = points.shape
    size, classes = beta.shape
    low, full = jnp.bfloat16, jnp.float32
    dma = pltpu.SemaphoreType.DMA
    vmem = pl.BlockSpec(memory_space=pltpu.VMEM)
    hbm = pl.BlockSpec(memory_space=pl.ANY)
    grad_t, logits_t = pl.pallas_call(
        functools.partial(body, n),
        name="falkon_step",
        out_shape=(
            jax.ShapeDtypeStruct((classes, size), full),
            jax.ShapeDtypeStruct((classes, rows), full),
        ),
        in_specs=[hbm, vmem, hbm, hbm, vmem, vmem],
        out_specs=(vmem, vmem),
        scratch_shapes=[
            pltpu.VMEM((n, size, size), low),
            pltpu.VMEM((chips, rows, features), low),
            pltpu.VMEM((2, size, features), low),
            pltpu.VMEM((chips, 2, size, rows), low),
            pltpu.VMEM((n, classes, size), low),
            pltpu.VMEM((2, classes, size), low),
            pltpu.VMEM((classes, size), full),
            pltpu.VMEM((chips, classes, rows), full),
            pltpu.VMEM((chips, classes, rows), full),
            pltpu.VMEM((chips, classes, rows), low),
            pltpu.VMEM((classes, size), full),
            pltpu.VMEM((classes, size), full),
            pltpu.VMEM((chips, classes, size), low),
            pltpu.VMEM((chips, classes, size), low),
            pltpu.VMEM((classes, size), full),
            pltpu.VMEM((chips, classes, size), full),
            pltpu.VMEM((chips, classes, size), full),
            pltpu.VMEM((chips, classes, size), full),
            dma((n,)),
            dma((2,)),
            dma((chips,)),
            dma((n,)),
            dma((chips,)),
            dma((3, chips, PIECES)),
            dma((chips, PIECES)),
            dma, dma, dma, dma,
            dma((chips,)),
            dma((chips,)),
            dma((chips,)),
            dma((chips,)),
            dma, dma,
            dma((chips,)),
            dma((chips,)),
            dma((chips,)),
            dma((chips,)),
        ],
        compiler_params=pltpu.CompilerParams(
            collective_id=0, has_side_effects=True, vmem_limit_bytes=60 * 1024 * 1024
        ),
    )(points, labels[None, :], centres, tri_inverse, beta.T, bias[None, :])
    grad_t, logits_t = pl.pallas_call(
        write_out,
        name="write_out",
        out_shape=(
            jax.ShapeDtypeStruct(grad_t.shape, full),
            jax.ShapeDtypeStruct(logits_t.shape, full),
        ),
        in_specs=[vmem, vmem],
        out_specs=(vmem, vmem),
    )(grad_t, logits_t)
    return grad_t.T, logits_t.T


def solution(mesh):
    return jax.shard_map(
        on_device,
        mesh=mesh,
        in_specs=(
            P(("groups", "pts"), None),
            P(("groups", "pts")),
            P(("groups", "pts"), None),
            P(("groups", "pts"), None),
            P(("groups", "pts"), None),
            P("groups"),
        ),
        out_specs=(P(("groups", "pts"), None), P(("groups", "pts"), None)),
        check_vma=False,
    )
```
